256 devices in a mesh: ctx: 32 (over y, z), head: 8 (over x, core).
Axes of the slice: x: 4, y: 4, z: 8, core: 2. Of those that a mesh axis runs over, the one named last changes fastest.
Arguments:
- mixer_input: bfloat16 [32768, 8192], P(('ctx', 'head')), may hold values from -0.0625 to 0.0625
- write_vectors: bfloat16 [32768, 1024], P(('ctx', 'head')), may hold values from -0.1875 to 0.1875
- read_vectors: bfloat16 [32768, 1024], P(('ctx', 'head')), may hold values from -0.1875 to 0.1875
- step_sizes: bfloat16 [32768, 128], P(('ctx', 'head')), may hold values from 0.5 to 22937
- fast_rates: float32 [128], replicated, may hold values from 1.5258789e-06 to 0.034
- slow_heads: int32 [64], replicated, may hold values from 0 to 127, as said below
- skip_gains: float32 [128], replicated, may hold values from 0.5 to 1.5
- mixer_grad: bfloat16 [32768, 8192], P(('ctx', 'head')), may hold values from -6 to 6
- queries: bfloat16 [32768, 4096], P(('ctx', 'head')), may hold values from -150 to 150
- attn_keys: bfloat16 [32768, 1024], P(('ctx', 'head')), may hold values from -6 to 6
- attn_values: bfloat16 [32768, 1024], P(('ctx', 'head')), may hold values from -24 to 24
- attn_grad: bfloat16 [32768, 4096], P(('ctx', 'head')), may hold values from -24 to 24
- doc_lengths: int32 [16], replicated, may hold values from 1 to 3072, 32768 in all
Outputs:
- grad_mixer_input: bfloat16 [32768, 8192], P(('ctx', 'head'))
- grad_write: bfloat16 [32768, 1024], P(('ctx', 'head'))
- grad_read: bfloat16 [32768, 1024], P(('ctx', 'head'))
- grad_queries: bfloat16 [32768, 4096], P(('ctx', 'head'))
The draws below stay inside these ranges and needn't reach their ends.
Inputs may be any that keep to these rules, and one draw needn't show every extreme that they name: `slow_heads`: distinct head numbers.
All inputs are finite; a program needn't handle non-finite values.
Results may differ from the reference program's by a relative error of at most 0.0062.
Values may be sent and summed in bfloat16 or wider, within the bound.
A program may use at most 192 MiB of HBM per device.

```python
import math
import jax
import jax.numpy as jnp
import numpy as np
from jax import lax

MH = 128
HD = 64
GROUPS = 8
NS = 128
QH = 32
KVH = 8
DH = 128
BLOCK = 256
DOCS = 16
SLOW = 64
SLAB_TOKENS = 32768
DOC_MOST = 3072


def paired_attention(key):
    base_offset = jax.random.fold_in(key, 7)
    keys_drawn = jnp.clip(jax.random.normal(jax.random.fold_in(base_offset, 1), (SLAB_TOKENS, KVH * DH), jnp.float32), -6.0, 6.0)
    queries_drawn = jnp.clip(jax.random.normal(jax.random.fold_in(base_offset, 2), (SLAB_TOKENS, QH * DH), jnp.float32), -6.0, 6.0)
    return (queries_drawn, keys_drawn)


def draw_queries(key, part):
    return paired_attention(key)[0].astype(jnp.bfloat16)


def draw_attn_keys(key, part):
    return paired_attention(key)[1].astype(jnp.bfloat16)


def draw_step_sizes(key, part):
    base_offset = jax.random.fold_in(key, 21)
    sampled_steps = jnp.exp(jax.random.uniform(jax.random.fold_in(base_offset, 1), (SLAB_TOKENS, MH), jnp.float32, math.log(0.5), math.log(2.0)))
    flurry_rows = jax.random.randint(jax.random.fold_in(base_offset, 2), (4,), 0, SLAB_TOKENS)
    flurry_lengths = jax.random.uniform(jax.random.fold_in(base_offset, 3), (4, 1), jnp.float32, 0.22, 0.69) * SLAB_TOKENS
    match_count = jnp.arange(SLAB_TOKENS)[None, :] == flurry_rows[:, None]
    flurry_groups = jnp.max(jnp.where(match_count, flurry_lengths, 0.0), axis=0)
    return jnp.maximum(sampled_steps, flurry_groups[:, None]).astype(jnp.bfloat16)


def draw_fast_rates(key, part):
    base_offset = jax.random.fold_in(key, 31)
    drawn = jnp.exp(jax.random.uniform(base_offset, (MH,), jnp.float32, math.log(1.0 / 50.0), math.log(1.0 / 30.0)))
    return drawn


def draw_slow_heads(key, part):
    return jax.random.permutation(jax.random.fold_in(key, 41), MH)[:SLOW].astype(jnp.int32)


def steps_of(stream_key, extent, split, least, high):
    def one(axis_at, parts):
        steps = jax.random.uniform(jax.random.fold_in(jax.random.fold_in(stream_key, 6), axis_at), (parts,), jnp.float32, least / len(split), high / len(split))
        return jnp.repeat(jnp.exp(steps), extent[axis_at] // parts).reshape((-1,) + (1,) * (len(extent) - axis_at - 1))

    gain = one(*split[0])
    for cut in split[1:]:
        gain = gain * one(*cut)
    return gain


def split_up(count, total, reach, skew):
    loads = [(1 << 20) // math.isqrt(rank ** skew) + 1 for rank in range(2, count + 1)]
    spare, counts = total - reach - (count - 1), [1] * (count - 1)
    while spare > 0:
        candidates = [i for i in range(count - 1) if counts[i] < reach]
        whole, remaining = sum([loads[i] for i in candidates]), spare
        for i in candidates:
            extra = min(reach - counts[i], max(1, remaining * loads[i] // whole), spare)
            counts[i] = counts[i] + extra
            spare = spare - extra
    return np.array([reach] + counts)


def uneven_parts(stream_key, amount, total, limit, skew):
    if amount == 2:
        one = jax.random.randint(stream_key, (), max(1, total - limit), min(limit, total - 1) + 1)
        return jnp.stack([one, total - one])
    sizes = jnp.asarray(split_up(amount, total, limit, skew), jnp.int32)
    twos = (amount - 1) // 2
    donor, sink = sizes[1:1 + 2 * twos:2], sizes[2:2 + 2 * twos:2]
    room = jnp.minimum(donor - 1, limit - sink)
    moved = jax.random.randint(jax.random.fold_in(stream_key, 1), (twos,), 0, 1 << 20) % (room + 1)
    sizes = sizes.at[1:1 + 2 * twos:2].set(donor - moved).at[2:2 + 2 * twos:2].set(sink + moved)
    return sizes[jax.random.permutation(jax.random.fold_in(stream_key, 2), amount)]


def normal_values(own_key, extent, width, bound, pieces=(), held_as=jnp.bfloat16):
    result = width * jax.random.normal(own_key, extent, jnp.float32)
    if pieces:
        result = result * steps_of(own_key, extent, pieces, -0.22, 0.18)
    return jnp.clip(result, -bound, bound).astype(held_as)


def setup_inputs(seed: int = 0) -> dict:
    key_of = jax.random.split(jax.random.key(seed), 14)
    return {
        "mixer_input": normal_values(key_of[0], (SLAB_TOKENS, MH * HD), 0.01, 0.0625, ((0, 256),)),
        "write_vectors": normal_values(key_of[1], (SLAB_TOKENS, GROUPS * NS), 0.03, 0.1875, ((0, 256),)),
        "read_vectors": normal_values(key_of[2], (SLAB_TOKENS, GROUPS * NS), 0.03, 0.1875, ((0, 256),)),
        "step_sizes": draw_step_sizes(jax.random.fold_in(key_of[13], 71), 0),
        "fast_rates": draw_fast_rates(jax.random.fold_in(key_of[13], 71), 0),
        "slow_heads": draw_slow_heads(jax.random.fold_in(key_of[13], 71), 0),
        "skip_gains": jnp.clip(jax.random.uniform(key_of[6], (MH,), jnp.float32, 0.5, 1.5), 0.5, 1.5),
        "mixer_grad": normal_values(key_of[7], (SLAB_TOKENS, MH * HD), 1.0, 6.0, ((0, 256),)),
        "queries": draw_queries(jax.random.fold_in(key_of[13], 71), 0),
        "attn_keys": draw_attn_keys(jax.random.fold_in(key_of[13], 71), 0),
        "attn_values": normal_values(key_of[10], (SLAB_TOKENS, KVH * DH), 4.0, 24.0, ((0, 256),)),
        "attn_grad": normal_values(key_of[11], (SLAB_TOKENS, QH * DH), 4.0, 24.0, ((0, 256),)),
        "doc_lengths": uneven_parts(key_of[12], DOCS, SLAB_TOKENS, DOC_MOST, 2).astype(jnp.int32),
    }


HIGH = lax.Precision.HIGHEST


def rounded(values):
    return lax.optimization_barrier(values.astype(jnp.bfloat16)).astype(jnp.float32)


def doc_index(positions, doc_lengths):
    starts = (jnp.cumsum(doc_lengths) - doc_lengths).astype(jnp.int32)
    match_count = (starts[None, :] <= positions[:, None]).astype(jnp.int32)
    return (jnp.sum(match_count, axis=1) - 1).astype(jnp.int32)


def stretch_edges_ref(stretch_inputs, stretch_write, stretch_read, decay_log, stretch_grads, docs, doc_prev):
    cumulative = jnp.cumsum(decay_log, axis=1)
    totals = cumulative[:, -1]
    linked = (docs == doc_prev[:, None]).astype(jnp.float32)
    tail_doc = (docs == docs[:, -1:]).astype(jnp.float32)
    stretch_links = jnp.exp(totals) * linked[:, -1][:, None, None]
    entering = jnp.exp(cumulative) * linked[:, :, None, None]
    to_end = jnp.exp(totals[:, None] - cumulative) * tail_doc[:, :, None, None]
    input_weighted = rounded(stretch_inputs * to_end[..., None])
    grad_weighted = rounded(stretch_grads * entering[..., None])
    endings = jnp.einsum("ksghp,ksgn->kghpn", input_weighted, stretch_write, precision=HIGH)
    openings = jnp.einsum("ktghp,ktgn->kghpn", grad_weighted, stretch_read, precision=HIGH)
    return cumulative, stretch_links, to_end, input_weighted, grad_weighted, endings, openings


def stretch_inner_ref(stretch_inputs, stretch_write, stretch_read, stretch_grads, docs, cumulative):
    block_rows = stretch_inputs.shape[1]
    offsets = jnp.arange(block_rows, dtype=jnp.int32)
    causal = offsets[:, None] >= offsets[None, :]
    same_doc = causal[None] & (docs[:, :, None] == docs[:, None, :])
    cum_heads = jnp.transpose(cumulative, (0, 2, 3, 1))
    log_gaps = cum_heads[..., :, None] - cum_heads[..., None, :]
    decays = jnp.exp(jnp.where(same_doc[:, None, None], log_gaps, -jnp.inf))
    scores = jnp.einsum("ktgn,ksgn->kgts", stretch_read, stretch_write, precision=HIGH)
    mixing = rounded(scores[:, :, None] * decays)
    input_inner = jnp.einsum("kghts,ktghp->ksghp", mixing, stretch_grads, precision=HIGH)
    inner_products = jnp.einsum("ktghp,ksghp->kghts", stretch_grads, stretch_inputs, precision=HIGH)
    joint_weights = rounded(jnp.sum(inner_products * decays, axis=2))
    read_inner = jnp.einsum("kgts,ksgn->ktgn", joint_weights, stretch_write, precision=HIGH)
    write_inner = jnp.einsum("kgts,ktgn->ksgn", joint_weights, stretch_read, precision=HIGH)
    return input_inner, write_inner, read_inner


def mixer_reference(mixer_input, write_vectors, read_vectors, step_sizes, fast_rates, slow_heads, skip_gains, mixer_grad, doc_lengths):
    per_group = MH // GROUPS
    stretch_count = SLAB_TOKENS // BLOCK
    head_ids = jnp.arange(MH, dtype=jnp.int32)
    slow_mask = jnp.any(head_ids[:, None] == slow_heads[None, :], axis=1)
    rates = jnp.where(slow_mask, 1.0 / SLAB_TOKENS, fast_rates).reshape(GROUPS, per_group)
    skip_here = skip_gains.reshape(GROUPS, per_group)
    shape_x = (stretch_count, 1, BLOCK, GROUPS, per_group, HD)
    shape_v = (stretch_count, 1, BLOCK, GROUPS, NS)
    positions = jnp.arange(SLAB_TOKENS, dtype=jnp.int32)
    docs = doc_index(positions, doc_lengths).reshape(stretch_count, 1, BLOCK)
    doc_prev = doc_index(positions[::BLOCK] - 1, doc_lengths).reshape(stretch_count, 1)
    decay_log = -step_sizes.astype(jnp.float32).reshape(stretch_count, 1, BLOCK, GROUPS, per_group) * rates
    items = (mixer_input.reshape(shape_x), write_vectors.reshape(shape_v), read_vectors.reshape(shape_v), decay_log, mixer_grad.reshape(shape_x), docs, doc_prev)

    def widen(element):
        return (element[0].astype(jnp.float32), element[1].astype(jnp.float32), element[2].astype(jnp.float32), element[3], element[4].astype(jnp.float32), element[5], element[6])

    def backward_step(carried, element):
        stretch_parts = stretch_edges_ref(*widen(element))
        return stretch_parts[6][0] + stretch_parts[1][0][..., None, None] * carried, carried

    zero_state = jnp.zeros((GROUPS, per_group, HD, NS), jnp.float32)
    unused, back_states = lax.scan(backward_step, zero_state, items, reverse=True)

    def forward_step(carried, element):
        stretch_inputs, stretch_write, stretch_read, stretch_decay, stretch_grads, stretch_docs, stretch_prev = widen(element[:7])
        back_state = rounded(element[7])
        state_low = rounded(carried)
        cumulative, stretch_links, to_end, input_weighted, grad_weighted, endings, openings = stretch_edges_ref(stretch_inputs, stretch_write, stretch_read, stretch_decay, stretch_grads, stretch_docs, stretch_prev)
        input_inner, write_inner, read_inner = stretch_inner_ref(stretch_inputs, stretch_write, stretch_read, stretch_grads, stretch_docs, cumulative)
        read_carried = jnp.einsum("ktghp,kghpn->ktgn", grad_weighted, state_low[None], precision=HIGH)
        write_carried = jnp.einsum("ksghp,kghpn->ksgn", input_weighted, back_state[None], precision=HIGH)
        input_carried = to_end[..., None] * jnp.einsum("ksgn,kghpn->ksghp", stretch_write, back_state[None], precision=HIGH)
        grad_input = (input_inner + input_carried + skip_here[..., None] * stretch_grads).astype(jnp.bfloat16)
        grad_write = (write_inner + write_carried).astype(jnp.bfloat16)
        grad_read = (read_inner + read_carried).astype(jnp.bfloat16)
        following = stretch_links[0][..., None, None] * carried + endings[0]
        return following, (grad_input, grad_write, grad_read)

    unused, outputs = lax.scan(forward_step, zero_state, items + (back_states,))
    return (outputs[0].reshape(SLAB_TOKENS, MH * HD), outputs[1].reshape(SLAB_TOKENS, GROUPS * NS), outputs[2].reshape(SLAB_TOKENS, GROUPS * NS))


def attend_ref(query_block, grad_block, key_block, value_block, query_pos, key_pos, query_doc, key_doc):
    scaling = DH ** -0.5
    logits = jnp.einsum("qgrd,kgd->grqk", query_block.astype(jnp.float32), key_block.astype(jnp.float32), precision=HIGH) * scaling
    allowed = (key_pos[None, :] <= query_pos[:, None]) & (key_pos[None, :] >= 0) & (query_doc[:, None] == key_doc[None, :])
    logits = jnp.where(allowed, logits, -jnp.inf)
    row_peaks = jnp.max(logits, axis=-1, keepdims=True)
    weights = jnp.exp(logits - row_peaks)
    probabilities = weights / jnp.sum(weights, axis=-1, keepdims=True)
    grad_probs = jnp.einsum("qgrd,kgd->grqk", grad_block.astype(jnp.float32), value_block.astype(jnp.float32), precision=HIGH)
    centre = jnp.sum(probabilities * grad_probs, axis=-1, keepdims=True)
    grad_logits = rounded(probabilities * (grad_probs - centre))
    return jnp.einsum("grqk,kgd->qgrd", grad_logits, key_block.astype(jnp.float32), precision=HIGH) * scaling


def attention_reference(queries, attn_keys, attn_values, attn_grad, doc_lengths):
    group_size = QH // KVH
    block_rows = min(128, SLAB_TOKENS)
    query_four = queries.reshape(SLAB_TOKENS, KVH, group_size, DH)
    grad_four = attn_grad.reshape(SLAB_TOKENS, KVH, group_size, DH)
    padding = jnp.zeros((DOC_MOST, KVH * DH), jnp.bfloat16)
    key_three = jnp.concatenate([padding, attn_keys], axis=0).reshape(DOC_MOST + SLAB_TOKENS, KVH, DH)
    value_three = jnp.concatenate([padding, attn_values], axis=0).reshape(DOC_MOST + SLAB_TOKENS, KVH, DH)
    query_positions = jnp.arange(SLAB_TOKENS, dtype=jnp.int32)
    key_positions = jnp.arange(SLAB_TOKENS + DOC_MOST, dtype=jnp.int32) - DOC_MOST
    query_docs = doc_index(query_positions, doc_lengths)
    key_docs = doc_index(key_positions, doc_lengths)

    def one_block(index):
        begin = (index * block_rows).astype(jnp.int32)
        span = DOC_MOST + block_rows
        return attend_ref(
            lax.dynamic_slice_in_dim(query_four, begin, block_rows, 0),
            lax.dynamic_slice_in_dim(grad_four, begin, block_rows, 0),
            lax.dynamic_slice_in_dim(key_three, begin, span, 0),
            lax.dynamic_slice_in_dim(value_three, begin, span, 0),
            lax.dynamic_slice_in_dim(query_positions, begin, block_rows, 0),
            lax.dynamic_slice_in_dim(key_positions, begin, span, 0),
            lax.dynamic_slice_in_dim(query_docs, begin, block_rows, 0),
            lax.dynamic_slice_in_dim(key_docs, begin, span, 0))

    blocks = lax.map(one_block, jnp.arange(SLAB_TOKENS // block_rows, dtype=jnp.int32))
    return blocks.reshape(SLAB_TOKENS, QH * DH).astype(jnp.bfloat16)


def reference(mixer_input, write_vectors, read_vectors, step_sizes, fast_rates, slow_heads, skip_gains, mixer_grad, queries, attn_keys, attn_values, attn_grad, doc_lengths):
    grad_input, grad_write, grad_read = mixer_reference(mixer_input, write_vectors, read_vectors, step_sizes, fast_rates, slow_heads, skip_gains, mixer_grad, doc_lengths)
    grad_queries = attention_reference(queries, attn_keys, attn_values, attn_grad, doc_lengths)
    return (grad_input, grad_write, grad_read, grad_queries)
```

```python
import functools

import jax
import jax.numpy as jnp
from jax import lax
from jax.experimental import pallas as pl
from jax.experimental.pallas import tpu as pltpu
from jax.sharding import Mesh
from jax.sharding import PartitionSpec as P

MH = 128
HD = 64
NS = 128
DH = 128
BLOCK = 256
LOG2E = 1.4426950408889634
REACH = 3
QB = 128
KB = 256
NEG = -1e30

F32 = jnp.float32
BF16 = jnp.bfloat16


def dot_nt(a, b):
    return lax.dot_general(a, b, (((1,), (1,)), ((), ())), preferred_element_type=F32)


def dot_nn(a, b):
    return lax.dot_general(a, b, (((1,), (0,)), ((), ())), preferred_element_type=F32)


def dot_tn(a, b):
    return lax.dot_general(a, b, (((0,), (0,)), ((), ())), preferred_element_type=F32)


def attention_kernel(starts, first, qg, kv_all, out, kv, s_scr, gp_scr, m_scr, l_scr, c_scr, acc, sems):
    i = pl.program_id(0)
    rows = kv.shape[0] // (REACH + 1)
    lead = REACH * rows
    docs = starts.shape[0]

    @pl.when(i == 0)
    def _():
        c = pltpu.make_async_copy(kv_all, kv, sems.at[0])
        c.start()
        c.wait()

    base = first[0] - lead
    q0 = first[0] + i * QB
    qcol = lead + i * QB + lax.broadcasted_iota(jnp.int32, (QB, 1), 0)
    dcol = jnp.zeros((QB, 1), jnp.int32)
    low = jnp.int32(0)
    for j in range(docs):
        st = starts[j]
        low = jnp.where(st <= q0, st, low)
        dcol = jnp.where(st - base <= qcol, st - base, dcol)
    first_block = (low - base) // KB
    blocks = (lead + i * QB + QB - 1) // KB - first_block + 1
    heads = out.shape[1] // DH
    q = jnp.concatenate([qg[:, h * DH : (h + 1) * DH] for h in range(heads)], axis=0)
    g = jnp.concatenate([qg[:, (heads + h) * DH : (heads + h + 1) * DH] for h in range(heads)], axis=0)
    m_scr[...] = jnp.full(m_scr.shape, NEG, F32)
    l_scr[...] = jnp.zeros(l_scr.shape, F32)
    c_scr[...] = jnp.zeros(c_scr.shape, F32)
    acc[...] = jnp.zeros(acc.shape, F32)

    def scores(b, _):
        r0 = pl.multiple_of((first_block + b) * KB, KB)
        k = kv[pl.ds(r0, KB), 0:DH]
        v = kv[pl.ds(r0, KB), DH : 2 * DH]
        key = r0 + lax.broadcasted_iota(jnp.int32, (QB, KB), 1)
        ok = (key >= dcol) & (key <= qcol)
        s = dot_nt(q, k)
        gp_scr[b] = dot_nt(g, v)
        for h in range(heads):
            sh = jnp.where(ok, s[h * QB : (h + 1) * QB], NEG)
            s_scr[b, h * QB : (h + 1) * QB, :] = sh
            top = m_scr[h * QB : (h + 1) * QB, :]
            for n in range(KB // 128):
                top = jnp.maximum(top, sh[:, n * 128 : (n + 1) * 128])
            m_scr[h * QB : (h + 1) * QB, :] = top
        return 0

    lax.fori_loop(0, blocks, scores, 0)
    scale = DH**-0.5 * LOG2E
    peak = jnp.max(m_scr[...], axis=1, keepdims=True)

    def weights(b, _):
        e = jnp.exp2((s_scr[b] - peak) * scale)
        s_scr[b] = e
        eg = e * gp_scr[b]
        l = l_scr[...]
        c = c_scr[...]
        for n in range(KB // 128):
            l += e[:, n * 128 : (n + 1) * 128]
            c += eg[:, n * 128 : (n + 1) * 128]
        l_scr[...] = l
        c_scr[...] = c
        return 0

    lax.fori_loop(0, blocks, weights, 0)
    total = jnp.sum(l_scr[...], axis=1, keepdims=True)
    centre = jnp.sum(c_scr[...], axis=1, keepdims=True) / total

    def grads(b, _):
        r0 = pl.multiple_of((first_block + b) * KB, KB)
        k = kv[pl.ds(r0, KB), 0:DH]
        ds = (s_scr[b] * (gp_scr[b] - centre)).astype(BF16)
        acc[...] += dot_nn(ds, k)
        return 0

    lax.fori_loop(0, blocks, grads, 0)
    res = (acc[...] * (DH**-0.5 / total)).astype(BF16)
    for h in range(heads):
        out[:, h * DH : (h + 1) * DH] = res[h * QB : (h + 1) * QB]


def attention(qg, kv, starts, first):
    rows = qg.shape[0]
    heads = qg.shape[1] // (2 * DH)
    lead = REACH * rows
    most = (lead + QB) // KB + 2
    hq = heads * QB
    return pl.pallas_call(
        attention_kernel,
        grid_spec=pltpu.PrefetchScalarGridSpec(
            num_scalar_prefetch=2,
            grid=(rows // QB,),
            in_specs=[pl.BlockSpec((QB, qg.shape[1]), lambda i, *_: (i, 0))]
            + [pl.BlockSpec(memory_space=pltpu.HBM)],
            out_specs=pl.BlockSpec((QB, heads * DH), lambda i, *_: (i, 0)),
            scratch_shapes=[
                pltpu.VMEM((lead + rows, 2 * DH), BF16),
                pltpu.VMEM((most, hq, KB), F32),
                pltpu.VMEM((most, hq, KB), F32),
                pltpu.VMEM((hq, 128), F32),
                pltpu.VMEM((hq, 128), F32),
                pltpu.VMEM((hq, 128), F32),
                pltpu.VMEM((hq, DH), F32),
                pltpu.SemaphoreType.DMA((1,)),
            ],
        ),
        out_shape=jax.ShapeDtypeStruct((rows, heads * DH), BF16),
        compiler_params=pltpu.CompilerParams(vmem_limit_bytes=56 << 20),
        cost_estimate=pl.CostEstimate(flops=12 * 10**9, bytes_accessed=6 << 20, transcendentals=16 * 10**6),
        name="attention",
    )(starts, first, qg, kv)


def split_sum(tri, dl):
    a = dl.astype(BF16)
    rest = dl - a.astype(F32)
    b = rest.astype(BF16)
    c = (rest - b.astype(F32)).astype(BF16)
    return dot_nn(tri, a) + dot_nn(tri, b) + dot_nn(tri, c)


def iota(shape, dim):
    return lax.broadcasted_iota(jnp.int32, shape, dim)


def doc_of(starts, pos):
    d = jnp.zeros(pos.shape, jnp.int32)
    for j in range(starts.shape[0]):
        d += (starts[j] <= pos).astype(jnp.int32)
    return d


def widen(values, spread):
    hi = values.astype(BF16)
    lo = (values - hi.astype(F32)).astype(BF16)
    return dot_nn(hi, spread) + dot_nn(lo, spread)


def edges(starts, first, c, st, rates):
    tri = (iota((BLOCK, BLOCK), 0) >= iota((BLOCK, BLOCK), 1)).astype(BF16)
    cum = split_sum(tri, st.astype(F32) * rates)
    begin = first + c * BLOCK
    doc_col = doc_of(starts, begin + iota((BLOCK, 1), 0))
    doc_last = doc_of(starts, begin + BLOCK - 1 + iota((1, 1), 0))
    doc_prev = doc_of(starts, begin - 1 + iota((1, 1), 0))
    total = cum[BLOCK - 1 : BLOCK, :]
    entering = jnp.exp2(jnp.where(doc_col == doc_prev, cum, NEG))
    to_end = jnp.exp2(jnp.where(doc_col == doc_last, total - cum, NEG))
    return cum, entering, to_end, doc_last == doc_prev


def spread_matrix(columns, group):
    return (iota((128, columns), 0) == group * (columns // HD) + iota((128, columns), 1) // HD).astype(BF16)


def edge_scratch(starts, first, st, rates, cum, cum_t, entering, to_end):
    @pl.when(pl.program_id(0) == 0)
    def _():
        a, b, c, _ = edges(starts, first[0], 0, st[...], rates[...])
        cum[...] = a
        cum_t[...] = jnp.transpose(a)
        entering[...] = b
        to_end[...] = c


MESH = pl.DeviceIdType.MESH


def links_of(rows):
    n = rows.shape[0] // 2
    return rows[0:n, :].astype(F32) + rows[n : 2 * n, :].astype(F32)


def first_kernel(
    starts, x, g, w, r, st, q, k, v, ag, rates,
    xs_out, gs_out, ws_out, rs_out, st_out, kv, qg, both,
    xs, gs, ws, rs, sts, ends_send, ends, lk, state, back, fs, fr, bs, br,
    own_sem, pair_send, pair_recv, head_send, head_recv, ends_ssem, ends_rsem, ring_ssem, ring_rsem, out_sem,
):
    ctx, hx, core = lax.axis_index("ctx"), lax.axis_index("hx"), lax.axis_index("core")
    slabs, chips, cores = lax.axis_size("ctx"), lax.axis_size("hx"), lax.axis_size("core")
    parts = chips * cores
    me = hx * cores + core
    other = 1 - core
    tokens = x.shape[0]
    rows = tokens * parts
    half = x.shape[1] // cores
    thin = w.shape[1] // cores
    qw = q.shape[1] // parts
    columns = half // chips
    heads = columns // HD
    begin = ctx * rows + hx * BLOCK

    def peer(d):
        p = lax.rem(me + d, parts)
        return p, {"hx": p // cores, "core": lax.rem(p, cores)}

    after = {"ctx": lax.rem(ctx + 1, slabs)}
    ahead = {"ctx": lax.rem(ctx + slabs - 1, slabs)}

    barrier = pltpu.get_barrier_semaphore()
    for d in range(1, parts):
        pl.semaphore_signal(barrier, inc=1, device_id=peer(d)[1], device_id_type=MESH)
    for n in (after, ahead):
        pl.semaphore_signal(barrier, inc=1, device_id=n, device_id_type=MESH)
    pl.semaphore_wait(barrier, parts + 1)

    def remote(src, dst, ssem, rsem, device):
        return pltpu.make_async_remote_copy(
            src_ref=src, dst_ref=dst, send_sem=ssem, recv_sem=rsem, device_id=device, device_id_type=MESH
        )

    def cols(n, width):
        return pl.ds(pl.multiple_of(n * width, 128), width)

    mine = pl.ds(pl.multiple_of(core * tokens, 128), tokens)
    pairs, owns = [], []
    for n, (src, dst, width) in enumerate(((x, xs, half), (g, gs, half), (w, ws, thin), (r, rs, thin), (st, sts, None))):
        theirs = src if width is None else src.at[:, cols(other, width)]
        ours = src if width is None else src.at[:, cols(core, width)]
        pairs.append(remote(theirs, dst.at[mine, :], pair_send.at[n], pair_recv.at[n], {"core": other}))
        owns.append(pltpu.make_async_copy(ours, dst.at[mine, :], own_sem.at[n]))
    for c in pairs + owns:
        c.start()
    lead = REACH * rows
    mine_kv = pl.ds(pl.multiple_of(lead + me * tokens, 128), tokens)
    mine_q = pl.ds(pl.multiple_of(me * tokens, 128), tokens)
    kv_moves, qg_moves, kv_own, qg_own = [], [], [], []
    for n, (src, dst, width, at, into, own) in enumerate(
        (
            (k, kv, DH, mine_kv, kv_moves, kv_own),
            (v, kv, DH, mine_kv, kv_moves, kv_own),
            (q, qg, qw, mine_q, qg_moves, qg_own),
            (ag, qg, qw, mine_q, qg_moves, qg_own),
        )
    ):
        place = slice((n % 2) * width, (n % 2 + 1) * width)
        for d in range(1, parts):
            p, device = peer(d)
            into.append(
                remote(src.at[:, cols(p, width)], dst.at[at, place], head_send.at[n, d], head_recv.at[n, d], device)
            )
        own.append(pltpu.make_async_copy(src.at[:, cols(me, width)], dst.at[at, place], own_sem.at[5 + n]))
    for c in kv_moves + kv_own + qg_own:
        c.start()

    for c in owns:
        c.wait()
    for c in pairs:
        c.wait_recv()
    outs = [
        pltpu.make_async_copy(src, dst, out_sem.at[n])
        for n, (src, dst) in enumerate(((xs, xs_out), (gs, gs_out), (ws, ws_out), (rs, rs_out), (sts, st_out)))
    ]
    for c in outs:
        c.start()

    cum, entering, to_end, linked = edges(starts, begin, 0, sts[...], rates[...])
    entering_hi = entering.astype(BF16)
    entering_lo = (entering - entering_hi.astype(F32)).astype(BF16)
    to_end_hi = to_end.astype(BF16)
    to_end_lo = (to_end - to_end_hi.astype(F32)).astype(BF16)
    tot = jnp.transpose(jnp.broadcast_to(cum[BLOCK - 1 : BLOCK, :], (128, 128)))
    link_all = jnp.exp2(jnp.where(linked, tot, NEG))

    def make_ends(group, out):
        spread = spread_matrix(columns, core * chips + group)
        wide_end = dot_nn(to_end_hi, spread) + dot_nn(to_end_lo, spread)
        wide_enter = dot_nn(entering_hi, spread) + dot_nn(entering_lo, spread)
        iw = (xs[:, cols(group, columns)].astype(F32) * wide_end).astype(BF16)
        gw = (gs[:, cols(group, columns)].astype(F32) * wide_enter).astype(BF16)
        out[0:columns, :] = dot_tn(iw, ws[:, cols(group, NS)]).astype(BF16)
        out[columns : 2 * columns, :] = dot_tn(gw, rs[:, cols(group, NS)]).astype(BF16)
        pick = (iota((heads, 128), 1) == (core * chips + group) * heads + iota((heads, 128), 0)).astype(F32)
        link = lax.dot_general(
            pick, link_all, (((1,), (0,)), ((), ())), precision=lax.Precision.HIGHEST, preferred_element_type=F32
        )
        hi = link.astype(BF16)
        out[2 * columns : 2 * columns + heads, :] = hi
        out[2 * columns + heads : 2 * columns + 2 * heads, :] = (link - hi.astype(F32)).astype(BF16)

    end_moves = []
    for d in range(1, chips):
        to = lax.rem(hx + d, chips)
        make_ends(to, ends_send.at[d - 1])
        c = remote(ends_send.at[d - 1], ends.at[hx], ends_ssem.at[d], ends_rsem.at[d], {"hx": to})
        c.start()
        end_moves.append(c)
    for c in qg_moves:
        c.start()
    make_ends(hx, ends.at[hx])

    for c in kv_own:
        c.wait()
    for c in kv_moves:
        c.wait_recv()
    hops = []
    for n in range(REACH):
        src = pl.ds((REACH - n) * rows, rows)
        dst = pl.ds((REACH - n - 1) * rows, rows)
        hops.append(remote(kv.at[src, :], kv.at[dst, :], ring_ssem.at[n], ring_rsem.at[n], after))
    for n in range(REACH):
        if n > 0:
            hops[n - 1].wait_recv()
        hops[n].start()

    for c in end_moves:
        c.wait_recv()
    for n in range(chips):
        lk[n] = links_of(ends[n, 2 * columns :, :])
    prods = [None, lk[0]]
    for n in range(1, chips):
        prods.append(prods[-1] * lk[n])
    for n in range(1, chips + 1):
        lk[chips + n - 1] = prods[n]
    whole = 2 * chips - 1

    def head_rows(h):
        return pl.ds(pl.multiple_of(h * HD, HD), HD), pl.ds(pl.multiple_of(columns + h * HD, HD), HD)

    def totals(h, _):
        at, bt = head_rows(h)
        one = pl.ds(h, 1)
        s = ends[0, at, :].astype(F32)
        b = ends[0, bt, :].astype(F32)
        for n in range(1, chips):
            s = lk[n, one, :] * s + ends[n, at, :].astype(F32)
            b = b + lk[chips + n - 1, one, :] * ends[n, bt, :].astype(F32)
        state[at, :] = s
        back[at, :] = b
        fs[0, at, :] = s.astype(BF16)
        bs[0, at, :] = b.astype(BF16)
        return 0

    lax.fori_loop(0, heads, totals, 0)
    fwd = [remote(fs.at[n], fr.at[n], ring_ssem.at[3 + n], ring_rsem.at[3 + n], after) for n in range(REACH)]
    bwd = [remote(bs.at[n], br.at[n], ring_ssem.at[6 + n], ring_rsem.at[6 + n], ahead) for n in range(REACH)]
    fwd[0].start()
    bwd[0].start()
    for n in range(1, REACH):
        for moves, base, recv, send in ((bwd, back, br, bs), (fwd, state, fr, fs)):
            moves[n - 1].wait_recv()

            def step(h, _):
                at, unused = head_rows(h)
                val = base[at, :] + lk[whole, pl.ds(h, 1), :] * recv[n - 1, at, :].astype(F32)
                send[n, at, :] = val.astype(BF16)
                return 0

            lax.fori_loop(0, heads, step, 0)
            moves[n].start()
    fwd[REACH - 1].wait_recv()
    bwd[REACH - 1].wait_recv()

    def chip_states(h, _):
        at, bt = head_rows(h)
        one = pl.ds(h, 1)
        s = fr[REACH - 1, at, :].astype(F32)
        b = br[REACH - 1, at, :].astype(F32)
        for n in range(chips):
            both[n, at, :] = s.astype(BF16)
            s = lk[n, one, :] * s + ends[n, at, :].astype(F32)
        for n in reversed(range(chips)):
            both[n, bt, :] = b.astype(BF16)
            b = lk[n, one, :] * b + ends[n, bt, :].astype(F32)
        return 0

    lax.fori_loop(0, heads, chip_states, 0)
    hops[REACH - 1].wait_recv()
    for c in qg_own + outs:
        c.wait()
    for c in qg_moves:
        c.wait_recv()
    for c in pairs + kv_moves + qg_moves + end_moves + hops + fwd + bwd:
        c.wait_send()


def first_stage(starts, x, g, w, r, st, q, k, v, ag, rates, parts, cores):
    chips = parts // cores
    tokens = x.shape[0]
    rows = tokens * parts
    half, thin = x.shape[1] // cores, w.shape[1] // cores
    columns = half // chips
    heads = columns // HD
    packed = 2 * columns + 2 * heads
    both_rows = cores * tokens
    hbm = pl.BlockSpec(memory_space=pltpu.HBM)
    vmem = pl.BlockSpec(memory_space=pltpu.VMEM)
    dma = pltpu.SemaphoreType.DMA
    return pl.pallas_call(
        first_kernel,
        in_specs=[pl.BlockSpec(memory_space=pltpu.SMEM)] + [hbm] * 9 + [vmem],
        out_specs=[hbm] * 7 + [vmem],
        out_shape=[
            jax.ShapeDtypeStruct((both_rows, half), BF16),
            jax.ShapeDtypeStruct((both_rows, half), BF16),
            jax.ShapeDtypeStruct((both_rows, thin), BF16),
            jax.ShapeDtypeStruct((both_rows, thin), BF16),
            jax.ShapeDtypeStruct((both_rows, st.shape[1]), BF16),
            jax.ShapeDtypeStruct(((REACH + 1) * rows, 2 * DH), BF16),
            jax.ShapeDtypeStruct((rows, 2 * q.shape[1] // parts), BF16),
            jax.ShapeDtypeStruct((chips, 2 * columns, NS), BF16),
        ],
        scratch_shapes=[
            pltpu.VMEM((both_rows, half), BF16),
            pltpu.VMEM((both_rows, half), BF16),
            pltpu.VMEM((both_rows, thin), BF16),
            pltpu.VMEM((both_rows, thin), BF16),
            pltpu.VMEM((both_rows, st.shape[1]), BF16),
            pltpu.VMEM((chips - 1, packed, NS), BF16),
            pltpu.VMEM((chips, packed, NS), BF16),
            pltpu.VMEM((2 * chips, heads, 128), F32),
            pltpu.VMEM((columns, NS), F32),
            pltpu.VMEM((columns, NS), F32),
            pltpu.VMEM((REACH, columns, NS), BF16),
            pltpu.VMEM((REACH, columns, NS), BF16),
            pltpu.VMEM((REACH, columns, NS), BF16),
            pltpu.VMEM((REACH, columns, NS), BF16),
            dma((9,)),
            dma((5,)),
            dma((5,)),
            dma((4, parts)),
            dma((4, parts)),
            dma((chips,)),
            dma((chips,)),
            dma((9,)),
            dma((9,)),
            dma((5,)),
        ],
        compiler_params=pltpu.CompilerParams(vmem_limit_bytes=60 << 20, collective_id=0, has_side_effects=True),
        cost_estimate=pl.CostEstimate(flops=2 * 10**9, bytes_accessed=16 << 20, transcendentals=10**5),
        name="first_stage",
    )(starts, x, g, w, r, st, q, k, v, ag, rates)


EDGES = [
    pltpu.VMEM((BLOCK, 128), F32),
    pltpu.VMEM((128, BLOCK), F32),
    pltpu.VMEM((BLOCK, 128), F32),
    pltpu.VMEM((BLOCK, 128), F32),
]


def grads_kernel(starts, first, core, x, g, w, r, st, rates, skips, both, out_x, out_w, out_r, cum, cum_t, entering, to_end):
    j = pl.program_id(0)
    columns = x.shape[1]
    heads = columns // HD
    edge_scratch(starts, first, st, rates, cum, cum_t, entering, to_end)
    begin = first[0]
    doc_col = doc_of(starts, begin + iota((BLOCK, 1), 0))
    doc_row = doc_of(starts, begin + iota((1, BLOCK), 1))
    ok = (iota((BLOCK, BLOCK), 0) <= iota((BLOCK, BLOCK), 1)) & (doc_col == doc_row)
    group = core[0] * pl.num_programs(0) + j
    spread = spread_matrix(columns, group)
    end_wide = widen(to_end[...], spread)
    iw = (x[...].astype(F32) * end_wide).astype(BF16)
    gw = (g[...].astype(F32) * widen(entering[...], spread)).astype(BF16)
    wv = w[...]
    rv = r[...]
    state = both[0, 0:columns, :]
    back = both[0, columns : 2 * columns, :]
    carried = dot_nt(wv, back)
    scores = dot_nt(wv, rv)
    joint = jnp.zeros((BLOCK, BLOCK), F32)
    lane = iota((BLOCK, 2 * HD), 1) < HD
    offset = pl.multiple_of(group * heads, heads)
    rows_t = cum_t[pl.ds(offset, heads), :]
    cols_all = jnp.transpose(jnp.concatenate([rows_t, jnp.zeros((128 - heads, BLOCK), F32)], axis=0))
    for p in range(heads // 2):
        cols = slice(p * 2 * HD, (p + 1) * 2 * HD)
        xp = x[:, cols]
        gp = g[:, cols]
        zero = jnp.zeros_like(xp)
        inner = skips[:, cols] * gp.astype(F32) + end_wide[:, cols] * carried[:, cols]
        for half in range(2):
            h = 2 * p + half
            mine = lane if half == 0 else ~lane
            decay = jnp.exp2(jnp.where(ok, rows_t[h : h + 1, :] - cols_all[:, h : h + 1], NEG))
            joint += decay * dot_nt(jnp.where(mine, xp, zero), gp)
            mixing = (scores * decay).astype(BF16)
            inner += dot_nn(mixing, jnp.where(mine, gp, zero))
        out_x[:, cols] = inner.astype(BF16)
    low = joint.astype(BF16)
    out_w[...] = (dot_nn(low, rv) + dot_nn(iw, back)).astype(BF16)
    out_r[...] = (dot_tn(low, wv) + dot_nn(gw, state)).astype(BF16)


def mixer_grads(mix, rates, skips, both, starts, first, core, columns, groups):
    return pl.pallas_call(
        grads_kernel,
        grid_spec=pltpu.PrefetchScalarGridSpec(
            num_scalar_prefetch=3,
            grid=(groups,),
            in_specs=[
                pl.BlockSpec((BLOCK, columns), lambda j, *_: (0, j)),
                pl.BlockSpec((BLOCK, columns), lambda j, *_: (0, j)),
                pl.BlockSpec((BLOCK, NS), lambda j, *_: (0, j)),
                pl.BlockSpec((BLOCK, NS), lambda j, *_: (0, j)),
                pl.BlockSpec((BLOCK, 128), lambda j, *_: (0, 0)),
                pl.BlockSpec((1, 128), lambda j, *_: (0, 0)),
                pl.BlockSpec((1, columns), lambda j, *_: (0, j)),
                pl.BlockSpec((1, 2 * columns, NS), lambda j, *_: (j, 0, 0)),
            ],
            out_specs=[
                pl.BlockSpec((BLOCK, columns), lambda j, *_: (0, j)),
                pl.BlockSpec((BLOCK, NS), lambda j, *_: (0, j)),
                pl.BlockSpec((BLOCK, NS), lambda j, *_: (0, j)),
            ],
            scratch_shapes=EDGES,
        ),
        out_shape=[
            jax.ShapeDtypeStruct((BLOCK, groups * columns), BF16),
            jax.ShapeDtypeStruct((BLOCK, groups * NS), BF16),
            jax.ShapeDtypeStruct((BLOCK, groups * NS), BF16),
        ],
        compiler_params=pltpu.CompilerParams(vmem_limit_bytes=40 << 20),
        cost_estimate=pl.CostEstimate(flops=8 * 10**9, bytes_accessed=14 << 20, transcendentals=5 * 10**6),
        name="mixer_grads",
    )(starts, first, core, *mix, rates, skips, both)


def unpack(moved):
    return moved.transpose(1, 0, 2).reshape(moved.shape[1], -1)


HEAD = ("hx", "core")


def shards(x, w, r, steps, fast_rates, slow_heads, skip_gains, grad, q, k, v, ag, doc_lengths):
    parts = lax.axis_size(HEAD)
    chips = lax.axis_size("hx")
    cores = lax.axis_size("core")
    tokens = x.shape[0]
    rows = tokens * parts
    columns = x.shape[1] // parts
    local_heads = MH // cores
    total_rows = rows * lax.axis_size("ctx")
    slab = (lax.axis_index("ctx") * rows).astype(jnp.int32)
    starts = (jnp.cumsum(doc_lengths) - doc_lengths).astype(jnp.int32)
    slab_first = slab.reshape(1)
    chip_first = (slab + lax.axis_index("hx") * BLOCK).astype(jnp.int32).reshape(1)

    slow = jnp.any(jnp.arange(MH, dtype=jnp.int32)[:, None] == slow_heads[None, :], axis=1)
    rates = jnp.where(slow, 1.0 / total_rows, fast_rates) * -LOG2E
    rates = rates.reshape(1, MH)
    core = lax.axis_index("core").astype(jnp.int32).reshape(1)
    skips = lax.dynamic_slice_in_dim(skip_gains, lax.axis_index("core") * local_heads, local_heads)
    skips = jnp.repeat(skips, HD).reshape(1, local_heads * HD)

    *mix, kv, qg, both = first_stage(starts, x, grad, w, r, steps, q, k, v, ag, rates, parts, cores)
    both = lax.all_to_all(both, "hx", split_axis=0, concat_axis=0, tiled=True)
    grad_q = attention(qg, kv, starts, slab_first)
    grad_q, both = lax.optimization_barrier((grad_q, both))
    moved = lax.all_to_all(grad_q, HEAD, split_axis=0, concat_axis=0, tiled=True)
    grad_q = unpack(moved.reshape(parts, tokens, -1))

    gx, gw, gr = mixer_grads(mix, rates, skips, both, starts, chip_first, core, columns, chips)
    joined = jnp.concatenate([gx, gw, gr], axis=1)
    moved = lax.all_to_all(joined, "core", split_axis=0, concat_axis=0, tiled=True)
    moved = moved.reshape(cores, tokens, -1)
    wide = local_heads * HD
    thin = chips * NS
    return (
        unpack(moved[:, :, :wide]),
        unpack(moved[:, :, wide : wide + thin]),
        unpack(moved[:, :, wide + thin :]),
        grad_q,
    )


def solution(mesh):
    split = Mesh(mesh.devices.reshape(mesh.shape["ctx"], -1, 2), ("ctx", "hx", "core"))
    tokens = P(("ctx", "hx", "core"), None)
    return jax.shard_map(
        shards,
        mesh=split,
        in_specs=(tokens, tokens, tokens, tokens, P(), P(), P(), tokens, tokens, tokens, tokens, tokens, P()),
        out_specs=(tokens, tokens, tokens, tokens),
        check_vma=False,
    )
```

```python
import functools

import jax
import jax.numpy as jnp
from jax import lax
from jax.experimental import pallas as pl
from jax.experimental.pallas import tpu as pltpu
from jax.sharding import Mesh
from jax.sharding import PartitionSpec as P

MH = 128
HD = 64
NS = 128
DH = 128
BLOCK = 256
LOG2E = 1.4426950408889634
REACH = 3
QB = 256
KB = 512
SUB = 256
NEG = -1e30

F32 = jnp.float32
BF16 = jnp.bfloat16


def dot_nt(a, b):
    return lax.dot_general(a, b, (((1,), (1,)), ((), ())), preferred_element_type=F32)


def dot_nn(a, b):
    return lax.dot_general(a, b, (((1,), (0,)), ((), ())), preferred_element_type=F32)


def dot_tn(a, b):
    return lax.dot_general(a, b, (((0,), (0,)), ((), ())), preferred_element_type=F32)


def attention_kernel(starts, first, qg, kv_all, out, kv, kt, turned, e_scr, gp_scr, tops, sems):
    i = pl.program_id(0)
    rows = kv_all.shape[0] // (REACH + 1)
    lead = REACH * rows
    docs = starts.shape[0]
    heads = out.shape[1] // DH

    @pl.when(i == 0)
    def _():
        c = pltpu.make_async_copy(kv_all, kv.at[pl.ds(KB, kv_all.shape[0]), :], sems.at[0])
        c.start()
        kv[0:KB, :] = jnp.zeros((KB, 2 * DH), BF16)
        c.wait()

        def turn(n, _):
            at = pl.ds(pl.multiple_of(n * KB, KB), KB)
            kt[:, at] = jnp.transpose(kv[at, 0:DH])
            return 0

        lax.fori_loop(0, kv.shape[0] // KB, turn, 0)

    for h in range(2 * heads):
        turned[h] = jnp.transpose(qg[:, h * DH : (h + 1) * DH])

    base = first[0] - lead
    q0 = lead + i * QB
    qrow = q0 + iota((1, QB), 1)
    drow = jnp.zeros((1, QB), jnp.int32)
    low = jnp.int32(0)
    high = jnp.int32(0)
    for j in range(docs):
        st = starts[j] - base
        low = jnp.where(st <= q0, st, low)
        high = jnp.where(st <= q0 + QB - 1, st, high)
        drow = jnp.where(st <= qrow, st, drow)
    end = q0 + QB
    blocks = (end - low + KB - 1) // KB
    begin = end - blocks * KB
    edge = blocks - 1
    full = jnp.minimum((high - begin + KB - 1) // KB, edge)
    scale = DH**-0.5 * LOG2E

    def fold(x):
        return x.reshape(-1, 8, QB)

    def place(b, n):
        return pl.ds(pl.multiple_of(KB + begin + b * KB + n * SUB, 128), SUB)

    def forward(masked, b, carry):
        new = []
        for h in range(heads):
            top, total, mean = carry[h]
            for n in range(KB // SUB):
                at = place(b, n)
                s = dot_nn(kv[at, 0:DH], turned[h])
                if masked:
                    key = begin + b * KB + n * SUB + iota((SUB, QB), 0)
                    s = jnp.where((key >= drow) & (key <= qrow), s, NEG)
                last = top
                top = jnp.maximum(top, jnp.max(jnp.max(fold(s), axis=0), axis=0, keepdims=True))
                e = jnp.exp2((s - top) * scale)
                gp = dot_nn(kv[at, DH : 2 * DH], turned[heads + h])
                part = slice(n * SUB, (n + 1) * SUB)
                e_scr[b, h, part, :] = e
                gp_scr[b, h, part, :] = gp
                tops[b, h, n] = jnp.broadcast_to(top, (8, QB))
                fade = jnp.exp2((last - top) * scale)
                total = total * fade + jnp.sum(fold(e), axis=0)
                mean = mean * fade + jnp.sum(fold(e * gp), axis=0)
            new.append((top, total, mean))
        return tuple(new)

    zero = jnp.zeros((8, QB), F32)
    carry = ((jnp.full((1, QB), NEG, F32), zero, zero),) * heads
    carry = lax.fori_loop(0, full, functools.partial(forward, True), carry)
    carry = lax.fori_loop(full, edge, functools.partial(forward, False), carry)
    carry = forward(True, edge, carry)
    peak = [c[0] for c in carry]
    total = [jnp.sum(c[1], axis=0, keepdims=True) for c in carry]
    centre = [jnp.sum(c[2], axis=0, keepdims=True) / t for c, t in zip(carry, total)]

    def grads(b, accs):
        new = []
        for h in range(heads):
            acc = accs[h]
            for n in range(KB // SUB):
                part = slice(n * SUB, (n + 1) * SUB)
                ds = (e_scr[b, h, part, :] * (gp_scr[b, h, part, :] - centre[h])).astype(BF16)
                fade = jnp.exp2((tops[b, h, n, 0:1, :] - peak[h]) * scale)
                acc += dot_nn(kt[:, place(b, n)], ds) * fade
            new.append(acc)
        return tuple(new)

    accs = lax.fori_loop(0, blocks, grads, (jnp.zeros((DH, QB), F32),) * heads)
    for h in range(heads):
        res = accs[h] * (DH**-0.5 / total[h])
        out[:, h * DH : (h + 1) * DH] = jnp.transpose(res).astype(BF16)


def attention(qg, kv, starts, first):
    rows = qg.shape[0]
    heads = qg.shape[1] // (2 * DH)
    lead = REACH * rows
    most = (lead + QB - 1 + KB - 1) // KB
    return pl.pallas_call(
        attention_kernel,
        grid_spec=pltpu.PrefetchScalarGridSpec(
            num_scalar_prefetch=2,
            grid=(rows // QB,),
            in_specs=[
                pl.BlockSpec((QB, qg.shape[1]), lambda i, *_: (i, 0)),
                pl.BlockSpec(memory_space=pltpu.HBM),
            ],
            out_specs=pl.BlockSpec((QB, heads * DH), lambda i, *_: (i, 0)),
            scratch_shapes=[
                pltpu.VMEM((KB + lead + rows, 2 * DH), BF16),
                pltpu.VMEM((DH, KB + lead + rows), BF16),
                pltpu.VMEM((2 * heads, DH, QB), BF16),
                pltpu.VMEM((most, heads, KB, QB), F32),
                pltpu.VMEM((most, heads, KB, QB), F32),
                pltpu.VMEM((most, heads, KB // SUB, 8, QB), F32),
                pltpu.SemaphoreType.DMA((1,)),
            ],
        ),
        out_shape=jax.ShapeDtypeStruct((rows, heads * DH), BF16),
        compiler_params=pltpu.CompilerParams(vmem_limit_bytes=58 << 20),
        cost_estimate=pl.CostEstimate(flops=12 * 10**9, bytes_accessed=6 << 20, transcendentals=16 * 10**6),
        name="attention",
    )(starts, first, qg, kv)


def split_sum(tri, dl):
    a = dl.astype(BF16)
    rest = dl - a.astype(F32)
    b = rest.astype(BF16)
    c = (rest - b.astype(F32)).astype(BF16)
    return dot_nn(tri, a) + dot_nn(tri, b) + dot_nn(tri, c)


def iota(shape, dim):
    return lax.broadcasted_iota(jnp.int32, shape, dim)


def doc_of(starts, pos):
    d = jnp.zeros(pos.shape, jnp.int32)
    for j in range(starts.shape[0]):
        d += (starts[j] <= pos).astype(jnp.int32)
    return d


def widen(values, spread):
    hi = values.astype(BF16)
    lo = (values - hi.astype(F32)).astype(BF16)
    return dot_nn(hi, spread) + dot_nn(lo, spread)


def edges(starts, first, c, st, rates):
    tri = (iota((BLOCK, BLOCK), 0) >= iota((BLOCK, BLOCK), 1)).astype(BF16)
    cum = split_sum(tri, st.astype(F32) * rates)
    begin = first + c * BLOCK
    doc_col = doc_of(starts, begin + iota((BLOCK, 1), 0))
    doc_last = doc_of(starts, begin + BLOCK - 1 + iota((1, 1), 0))
    doc_prev = doc_of(starts, begin - 1 + iota((1, 1), 0))
    total = cum[BLOCK - 1 : BLOCK, :]
    entering = jnp.exp2(jnp.where(doc_col == doc_prev, cum, NEG))
    to_end = jnp.exp2(jnp.where(doc_col == doc_last, total - cum, NEG))
    return cum, entering, to_end, doc_last == doc_prev


def spread_matrix(columns, group):
    return (iota((128, columns), 0) == group * (columns // HD) + iota((128, columns), 1) // HD).astype(BF16)


def edge_scratch(starts, first, st, rates, cum, cum_t, entering, to_end):
    @pl.when(pl.program_id(0) == 0)
    def _():
        a, b, c, _ = edges(starts, first[0], 0, st[...], rates[...])
        cum[...] = a
        cum_t[...] = jnp.transpose(a)
        entering[...] = b
        to_end[...] = c


MESH = pl.DeviceIdType.MESH


def links_of(rows):
    n = rows.shape[0] // 2
    return rows[0:n, :].astype(F32) + rows[n : 2 * n, :].astype(F32)


def first_kernel(
    starts, x, g, w, r, st, q, k, v, ag, rates,
    xs_out, gs_out, ws_out, rs_out, st_out, kv, qg, both,
    xs, gs, ws, rs, sts, ends_send, ends, lk, state, back, fs, fr, bs, br,
    own_sem, pair_send, pair_recv, head_send, head_recv, ends_ssem, ends_rsem, ring_ssem, ring_rsem, out_sem,
):
    ctx, hx, core = lax.axis_index("ctx"), lax.axis_index("hx"), lax.axis_index("core")
    slabs, chips, cores = lax.axis_size("ctx"), lax.axis_size("hx"), lax.axis_size("core")
    parts = chips * cores
    me = hx * cores + core
    other = 1 - core
    tokens = x.shape[0]
    rows = tokens * parts
    half = x.shape[1] // cores
    thin = w.shape[1] // cores
    qw = q.shape[1] // parts
    columns = half // chips
    heads = columns // HD
    begin = ctx * rows + hx * BLOCK

    def peer(d):
        p = lax.rem(me + d, parts)
        return p, {"hx": p // cores, "core": lax.rem(p, cores)}

    after = {"ctx": lax.rem(ctx + 1, slabs)}
    ahead = {"ctx": lax.rem(ctx + slabs - 1, slabs)}

    barrier = pltpu.get_barrier_semaphore()
    for d in range(1, parts):
        pl.semaphore_signal(barrier, inc=1, device_id=peer(d)[1], device_id_type=MESH)
    for n in (after, ahead):
        pl.semaphore_signal(barrier, inc=1, device_id=n, device_id_type=MESH)
    pl.semaphore_wait(barrier, parts + 1)

    def remote(src, dst, ssem, rsem, device):
        return pltpu.make_async_remote_copy(
            src_ref=src, dst_ref=dst, send_sem=ssem, recv_sem=rsem, device_id=device, device_id_type=MESH
        )

    def cols(n, width):
        return pl.ds(pl.multiple_of(n * width, 128), width)

    mine = pl.ds(pl.multiple_of(core * tokens, 128), tokens)
    pairs, owns = [], []
    for n, (src, dst, width) in enumerate(((x, xs, half), (g, gs, half), (w, ws, thin), (r, rs, thin), (st, sts, None))):
        theirs = src if width is None else src.at[:, cols(other, width)]
        ours = src if width is None else src.at[:, cols(core, width)]
        pairs.append(remote(theirs, dst.at[mine, :], pair_send.at[n], pair_recv.at[n], {"core": other}))
        owns.append(pltpu.make_async_copy(ours, dst.at[mine, :], own_sem.at[n]))
    for c in pairs + owns:
        c.start()
    lead = REACH * rows
    mine_kv = pl.ds(pl.multiple_of(lead + me * tokens, 128), tokens)
    mine_q = pl.ds(pl.multiple_of(me * tokens, 128), tokens)
    kv_moves, qg_moves, kv_own, qg_own = [], [], [], []
    for n, (src, dst, width, at, into, own) in enumerate(
        (
            (k, kv, DH, mine_kv, kv_moves, kv_own),
            (v, kv, DH, mine_kv, kv_moves, kv_own),
            (q, qg, qw, mine_q, qg_moves, qg_own),
            (ag, qg, qw, mine_q, qg_moves, qg_own),
        )
    ):
        place = slice((n % 2) * width, (n % 2 + 1) * width)
        for d in range(1, parts):
            p, device = peer(d)
            into.append(
                remote(src.at[:, cols(p, width)], dst.at[at, place], head_send.at[n, d], head_recv.at[n, d], device)
            )
        own.append(pltpu.make_async_copy(src.at[:, cols(me, width)], dst.at[at, place], own_sem.at[5 + n]))
    for c in kv_moves + kv_own + qg_own:
        c.start()

    for c in owns:
        c.wait()
    for c in pairs:
        c.wait_recv()
    outs = [
        pltpu.make_async_copy(src, dst, out_sem.at[n])
        for n, (src, dst) in enumerate(((xs, xs_out), (gs, gs_out), (ws, ws_out), (rs, rs_out), (sts, st_out)))
    ]
    for c in outs:
        c.start()

    cum, entering, to_end, linked = edges(starts, begin, 0, sts[...], rates[...])
    entering_hi = entering.astype(BF16)
    entering_lo = (entering - entering_hi.astype(F32)).astype(BF16)
    to_end_hi = to_end.astype(BF16)
    to_end_lo = (to_end - to_end_hi.astype(F32)).astype(BF16)
    tot = jnp.transpose(jnp.broadcast_to(cum[BLOCK - 1 : BLOCK, :], (128, 128)))
    link_all = jnp.exp2(jnp.where(linked, tot, NEG))

    def make_ends(group, out):
        spread = spread_matrix(columns, core * chips + group)
        wide_end = dot_nn(to_end_hi, spread) + dot_nn(to_end_lo, spread)
        wide_enter = dot_nn(entering_hi, spread) + dot_nn(entering_lo, spread)
        iw = (xs[:, cols(group, columns)].astype(F32) * wide_end).astype(BF16)
        gw = (gs[:, cols(group, columns)].astype(F32) * wide_enter).astype(BF16)
        out[0:columns, :] = dot_tn(iw, ws[:, cols(group, NS)]).astype(BF16)
        out[columns : 2 * columns, :] = dot_tn(gw, rs[:, cols(group, NS)]).astype(BF16)
        pick = (iota((heads, 128), 1) == (core * chips + group) * heads + iota((heads, 128), 0)).astype(F32)
        link = lax.dot_general(
            pick, link_all, (((1,), (0,)), ((), ())), precision=lax.Precision.HIGHEST, preferred_element_type=F32
        )
        hi = link.astype(BF16)
        out[2 * columns : 2 * columns + heads, :] = hi
        out[2 * columns + heads : 2 * columns + 2 * heads, :] = (link - hi.astype(F32)).astype(BF16)

    end_moves = []
    for d in range(1, chips):
        to = lax.rem(hx + d, chips)
        make_ends(to, ends_send.at[d - 1])
        c = remote(ends_send.at[d - 1], ends.at[hx], ends_ssem.at[d], ends_rsem.at[d], {"hx": to})
        c.start()
        end_moves.append(c)
    make_ends(hx, ends.at[hx])

    for c in kv_own:
        c.wait()
    for c in kv_moves:
        c.wait_recv()
    hops = []
    for n in range(REACH):
        src = pl.ds((REACH - n) * rows, rows)
        dst = pl.ds((REACH - n - 1) * rows, rows)
        hops.append(remote(kv.at[src, :], kv.at[dst, :], ring_ssem.at[n], ring_rsem.at[n], after))
    for n in range(REACH):
        if n > 0:
            hops[n - 1].wait_recv()
        hops[n].start()

    for c in end_moves:
        c.wait_recv()
    for c in qg_moves:
        c.start()
    for n in range(chips):
        lk[n] = links_of(ends[n, 2 * columns :, :])
    prods = [None, lk[0]]
    for n in range(1, chips):
        prods.append(prods[-1] * lk[n])
    for n in range(1, chips + 1):
        lk[chips + n - 1] = prods[n]
    whole = 2 * chips - 1

    def head_rows(h):
        return pl.ds(pl.multiple_of(h * HD, HD), HD), pl.ds(pl.multiple_of(columns + h * HD, HD), HD)

    def totals(h, _):
        at, bt = head_rows(h)
        one = pl.ds(h, 1)
        s = ends[0, at, :].astype(F32)
        b = ends[0, bt, :].astype(F32)
        for n in range(1, chips):
            s = lk[n, one, :] * s + ends[n, at, :].astype(F32)
            b = b + lk[chips + n - 1, one, :] * ends[n, bt, :].astype(F32)
        state[at, :] = s
        back[at, :] = b
        fs[0, at, :] = s.astype(BF16)
        bs[0, at, :] = b.astype(BF16)
        return 0

    lax.fori_loop(0, heads, totals, 0)
    fwd = [remote(fs.at[n], fr.at[n], ring_ssem.at[3 + n], ring_rsem.at[3 + n], after) for n in range(REACH)]
    bwd = [remote(bs.at[n], br.at[n], ring_ssem.at[6 + n], ring_rsem.at[6 + n], ahead) for n in range(REACH)]
    fwd[0].start()
    bwd[0].start()
    for n in range(1, REACH):
        for moves, base, recv, send in ((bwd, back, br, bs), (fwd, state, fr, fs)):
            moves[n - 1].wait_recv()

            def step(h, _):
                at, unused = head_rows(h)
                val = base[at, :] + lk[whole, pl.ds(h, 1), :] * recv[n - 1, at, :].astype(F32)
                send[n, at, :] = val.astype(BF16)
                return 0

            lax.fori_loop(0, heads, step, 0)
            moves[n].start()
    fwd[REACH - 1].wait_recv()
    bwd[REACH - 1].wait_recv()

    def chip_states(h, _):
        at, bt = head_rows(h)
        one = pl.ds(h, 1)
        s = fr[REACH - 1, at, :].astype(F32)
        b = br[REACH - 1, at, :].astype(F32)
        for n in range(chips):
            both[n, at, :] = s.astype(BF16)
            s = lk[n, one, :] * s + ends[n, at, :].astype(F32)
        for n in reversed(range(chips)):
            both[n, bt, :] = b.astype(BF16)
            b = lk[n, one, :] * b + ends[n, bt, :].astype(F32)
        return 0

    lax.fori_loop(0, heads, chip_states, 0)
    hops[REACH - 1].wait_recv()
    for c in qg_own + outs:
        c.wait()
    for c in qg_moves:
        c.wait_recv()
    for c in pairs + kv_moves + qg_moves + end_moves + hops + fwd + bwd:
        c.wait_send()


def first_stage(starts, x, g, w, r, st, q, k, v, ag, rates, parts, cores):
    chips = parts // cores
    tokens = x.shape[0]
    rows = tokens * parts
    half, thin = x.shape[1] // cores, w.shape[1] // cores
    columns = half // chips
    heads = columns // HD
    packed = 2 * columns + 2 * heads
    both_rows = cores * tokens
    hbm = pl.BlockSpec(memory_space=pltpu.HBM)
    vmem = pl.BlockSpec(memory_space=pltpu.VMEM)
    dma = pltpu.SemaphoreType.DMA
    return pl.pallas_call(
        first_kernel,
        in_specs=[pl.BlockSpec(memory_space=pltpu.SMEM)] + [hbm] * 9 + [vmem],
        out_specs=[hbm] * 7 + [vmem],
        out_shape=[
            jax.ShapeDtypeStruct((both_rows, half), BF16),
            jax.ShapeDtypeStruct((both_rows, half), BF16),
            jax.ShapeDtypeStruct((both_rows, thin), BF16),
            jax.ShapeDtypeStruct((both_rows, thin), BF16),
            jax.ShapeDtypeStruct((both_rows, st.shape[1]), BF16),
            jax.ShapeDtypeStruct(((REACH + 1) * rows, 2 * DH), BF16),
            jax.ShapeDtypeStruct((rows, 2 * q.shape[1] // parts), BF16),
            jax.ShapeDtypeStruct((chips, 2 * columns, NS), BF16),
        ],
        scratch_shapes=[
            pltpu.VMEM((both_rows, half), BF16),
            pltpu.VMEM((both_rows, half), BF16),
            pltpu.VMEM((both_rows, thin), BF16),
            pltpu.VMEM((both_rows, thin), BF16),
            pltpu.VMEM((both_rows, st.shape[1]), BF16),
            pltpu.VMEM((chips - 1, packed, NS), BF16),
            pltpu.VMEM((chips, packed, NS), BF16),
            pltpu.VMEM((2 * chips, heads, 128), F32),
            pltpu.VMEM((columns, NS), F32),
            pltpu.VMEM((columns, NS), F32),
            pltpu.VMEM((REACH, columns, NS), BF16),
            pltpu.VMEM((REACH, columns, NS), BF16),
            pltpu.VMEM((REACH, columns, NS), BF16),
            pltpu.VMEM((REACH, columns, NS), BF16),
            dma((9,)),
            dma((5,)),
            dma((5,)),
            dma((4, parts)),
            dma((4, parts)),
            dma((chips,)),
            dma((chips,)),
            dma((9,)),
            dma((9,)),
            dma((5,)),
        ],
        compiler_params=pltpu.CompilerParams(vmem_limit_bytes=60 << 20, collective_id=0, has_side_effects=True),
        cost_estimate=pl.CostEstimate(flops=2 * 10**9, bytes_accessed=16 << 20, transcendentals=10**5),
        name="first_stage",
    )(starts, x, g, w, r, st, q, k, v, ag, rates)


EDGES = [
    pltpu.VMEM((BLOCK, 128), F32),
    pltpu.VMEM((128, BLOCK), F32),
    pltpu.VMEM((BLOCK, 128), F32),
    pltpu.VMEM((BLOCK, 128), F32),
]


def last_kernel(
    starts, x, g, w, r, st, rates, skips, both, grad_q, out_x, out_w, out_r, out_q,
    cum, cum_t, entering, to_end, res_x, res_w, res_r, own_sem, pair_send, pair_recv, q_send, q_recv,
):
    j = pl.program_id(0)
    ctx, hx, core = lax.axis_index("ctx"), lax.axis_index("hx"), lax.axis_index("core")
    chips, cores = lax.axis_size("hx"), lax.axis_size("core")
    parts = chips * cores
    me = hx * cores + core
    other = 1 - core
    tokens = out_x.shape[0]
    columns = x.shape[1]
    heads = columns // HD
    qw = grad_q.shape[1]
    begin = ctx * tokens * parts + hx * BLOCK
    group = core * chips + j

    def cols(n, width):
        return pl.ds(pl.multiple_of(n * width, 128), width)

    def remote(src, dst, ssem, rsem, device):
        return pltpu.make_async_remote_copy(
            src_ref=src, dst_ref=dst, send_sem=ssem, recv_sem=rsem, device_id=device, device_id_type=MESH
        )

    def q_moves():
        moves = []
        for d in range(1, parts):
            p = lax.rem(me + d, parts)
            device = {"hx": p // cores, "core": lax.rem(p, cores)}
            moves.append(remote(grad_q.at[cols(p, tokens), :], out_q.at[:, cols(me, qw)], q_send.at[d], q_recv.at[d], device))
        own = pltpu.make_async_copy(grad_q.at[cols(me, tokens), :], out_q.at[:, cols(me, qw)], own_sem.at[chips, 0])
        return moves, own

    def pair_moves(n):
        moves, owns = [], []
        for k, (res, out, width) in enumerate(((res_x, out_x, columns), (res_w, out_w, NS), (res_r, out_r, NS))):
            place = out.at[:, cols(core * chips + n, width)]
            moves.append(
                remote(res.at[n, cols(other, tokens), :], place, pair_send.at[n, k], pair_recv.at[n, k], {"core": other})
            )
            owns.append(pltpu.make_async_copy(res.at[n, cols(core, tokens), :], place, own_sem.at[n, k]))
        return moves, owns

    @pl.when(j == 0)
    def _():
        barrier = pltpu.get_barrier_semaphore()
        for d in range(1, parts):
            p = lax.rem(me + d, parts)
            pl.semaphore_signal(
                barrier, inc=1, device_id={"hx": p // cores, "core": lax.rem(p, cores)}, device_id_type=MESH
            )
        pl.semaphore_wait(barrier, parts - 1)
        moves, own = q_moves()
        for c in moves + [own]:
            c.start()
        a, b, c, _ = edges(starts, begin, 0, st[...], rates[...])
        cum[...] = a
        cum_t[...] = jnp.transpose(a)
        entering[...] = b
        to_end[...] = c

    doc_col = doc_of(starts, begin + iota((BLOCK, 1), 0))
    doc_row = doc_of(starts, begin + iota((1, BLOCK), 1))
    ok = (iota((BLOCK, BLOCK), 0) <= iota((BLOCK, BLOCK), 1)) & (doc_col == doc_row)
    spread = spread_matrix(columns, group)
    end_wide = widen(to_end[...], spread)
    iw = (x[...].astype(F32) * end_wide).astype(BF16)
    gw = (g[...].astype(F32) * widen(entering[...], spread)).astype(BF16)
    wv = w[...]
    rv = r[...]
    state = both[0, 0:columns, :]
    back = both[0, columns : 2 * columns, :]
    carried = dot_nt(wv, back)
    scores = dot_nt(wv, rv)
    joint = jnp.zeros((BLOCK, BLOCK), F32)
    lane = iota((BLOCK, 2 * HD), 1) < HD
    offset = pl.multiple_of(group * heads, heads)
    rows_t = cum_t[pl.ds(offset, heads), :]
    cols_all = jnp.transpose(jnp.concatenate([rows_t, jnp.zeros((128 - heads, BLOCK), F32)], axis=0))
    for p in range(heads // 2):
        at = slice(p * 2 * HD, (p + 1) * 2 * HD)
        xp = x[:, at]
        gp = g[:, at]
        zero = jnp.zeros_like(xp)
        inner = skips[:, at] * gp.astype(F32) + end_wide[:, at] * carried[:, at]
        for half in range(2):
            h = 2 * p + half
            mine = lane if half == 0 else ~lane
            decay = jnp.exp2(jnp.where(ok, rows_t[h : h + 1, :] - cols_all[:, h : h + 1], NEG))
            joint += decay * dot_nt(jnp.where(mine, xp, zero), gp)
            mixing = (scores * decay).astype(BF16)
            inner += dot_nn(mixing, jnp.where(mine, gp, zero))
        res_x[j, :, at] = inner.astype(BF16)
    low = joint.astype(BF16)
    res_w[j] = (dot_nn(low, rv) + dot_nn(iw, back)).astype(BF16)
    res_r[j] = (dot_tn(low, wv) + dot_nn(gw, state)).astype(BF16)

    for n in range(chips):

        @pl.when(j == n)
        def _():
            moves, owns = pair_moves(n)
            for c in moves + owns:
                c.start()

    @pl.when(j == chips - 1)
    def _():
        moves, own = q_moves()
        own.wait()
        for c in moves:
            c.wait_recv()
        for c in moves:
            c.wait_send()
        for n in range(chips):
            moves, owns = pair_moves(n)
            for c in owns:
                c.wait()
            for c in moves:
                c.wait_recv()
            for c in moves:
                c.wait_send()


def last_stage(mix, rates, skips, both, starts, grad_q, parts, cores):
    chips = both.shape[0]
    columns = both.shape[1] // 2
    tokens = BLOCK // cores
    groups = chips * cores
    hbm = pl.BlockSpec(memory_space=pltpu.HBM)
    dma = pltpu.SemaphoreType.DMA
    return pl.pallas_call(
        last_kernel,
        grid_spec=pltpu.PrefetchScalarGridSpec(
            num_scalar_prefetch=1,
            grid=(chips,),
            in_specs=[
                pl.BlockSpec((BLOCK, columns), lambda j, *_: (0, j)),
                pl.BlockSpec((BLOCK, columns), lambda j, *_: (0, j)),
                pl.BlockSpec((BLOCK, NS), lambda j, *_: (0, j)),
                pl.BlockSpec((BLOCK, NS), lambda j, *_: (0, j)),
                pl.BlockSpec((BLOCK, 128), lambda j, *_: (0, 0)),
                pl.BlockSpec((1, 128), lambda j, *_: (0, 0)),
                pl.BlockSpec((1, columns), lambda j, *_: (0, j)),
                pl.BlockSpec((1, 2 * columns, NS), lambda j, *_: (j, 0, 0)),
                hbm,
            ],
            out_specs=[hbm] * 4,
            scratch_shapes=EDGES
            + [
                pltpu.VMEM((chips, BLOCK, columns), BF16),
                pltpu.VMEM((chips, BLOCK, NS), BF16),
                pltpu.VMEM((chips, BLOCK, NS), BF16),
                dma((chips + 1, 3)),
                dma((chips, 3)),
                dma((chips, 3)),
                dma((parts,)),
                dma((parts,)),
            ],
        ),
        out_shape=[
            jax.ShapeDtypeStruct((tokens, groups * columns), BF16),
            jax.ShapeDtypeStruct((tokens, groups * NS), BF16),
            jax.ShapeDtypeStruct((tokens, groups * NS), BF16),
            jax.ShapeDtypeStruct((tokens, parts * grad_q.shape[1]), BF16),
        ],
        compiler_params=pltpu.CompilerParams(vmem_limit_bytes=56 << 20, collective_id=1, has_side_effects=True),
        cost_estimate=pl.CostEstimate(flops=8 * 10**9, bytes_accessed=14 << 20, transcendentals=5 * 10**6),
        name="last_stage",
    )(starts, *mix, rates, skips, both, grad_q)


HEAD = ("hx", "core")


def shards(x, w, r, steps, fast_rates, slow_heads, skip_gains, grad, q, k, v, ag, doc_lengths):
    parts = lax.axis_size(HEAD)
    chips = lax.axis_size("hx")
    cores = lax.axis_size("core")
    tokens = x.shape[0]
    rows = tokens * parts
    columns = x.shape[1] // parts
    local_heads = MH // cores
    total_rows = rows * lax.axis_size("ctx")
    slab = (lax.axis_index("ctx") * rows).astype(jnp.int32)
    starts = (jnp.cumsum(doc_lengths) - doc_lengths).astype(jnp.int32)
    slab_first = slab.reshape(1)

    slow = jnp.any(jnp.arange(MH, dtype=jnp.int32)[:, None] == slow_heads[None, :], axis=1)
    rates = jnp.where(slow, 1.0 / total_rows, fast_rates) * -LOG2E
    rates = rates.reshape(1, MH)
    skips = lax.dynamic_slice_in_dim(skip_gains, lax.axis_index("core") * local_heads, local_heads)
    skips = jnp.repeat(skips, HD).reshape(1, local_heads * HD)

    *mix, kv, qg, both = first_stage(starts, x, grad, w, r, steps, q, k, v, ag, rates, parts, cores)
    both = lax.all_to_all(both, "hx", split_axis=0, concat_axis=0, tiled=True)
    grad_q = attention(qg, kv, starts, slab_first)
    return tuple(last_stage(mix, rates, skips, both, starts, grad_q, parts, cores))


def solution(mesh):
    split = Mesh(mesh.devices.reshape(mesh.shape["ctx"], -1, 2), ("ctx", "hx", "core"))
    tokens = P(("ctx", "hx", "core"), None)
    return jax.shard_map(
        shards,
        mesh=split,
        in_specs=(tokens, tokens, tokens, tokens, P(), P(), P(), tokens, tokens, tokens, tokens, tokens, P()),
        out_specs=(tokens, tokens, tokens, tokens),
        check_vma=False,
    )
```

```python
import functools

import jax
import jax.numpy as jnp
from jax import lax
from jax.experimental import pallas as pl
from jax.experimental.pallas import tpu as pltpu
from jax.sharding import Mesh
from jax.sharding import PartitionSpec as P

MH = 128
HD = 64
NS = 128
DH = 128
BLOCK = 256
LOG2E = 1.4426950408889634
REACH = 3
QB = 256
KB = 512
SUB = 256
EARLY = 3
NEG = -1e30

F32 = jnp.float32
BF16 = jnp.bfloat16


def dot_nt(a, b):
    return lax.dot_general(a, b, (((1,), (1,)), ((), ())), preferred_element_type=F32)


def dot_nn(a, b):
    return lax.dot_general(a, b, (((1,), (0,)), ((), ())), preferred_element_type=F32)


def dot_tn(a, b):
    return lax.dot_general(a, b, (((0,), (0,)), ((), ())), preferred_element_type=F32)


def attention_kernel(lengths, first, qg, kv_all, out, kv, kt, turned, e_scr, gp_scr, tops, sems):
    i = pl.program_id(0)
    rows = kv_all.shape[0] // (REACH + 1)
    lead = REACH * rows
    heads = out.shape[1] // DH

    @pl.when(i == 0)
    def _():
        c = pltpu.make_async_copy(kv_all, kv.at[pl.ds(KB, kv_all.shape[0]), :], sems.at[0])
        c.start()
        kv[0:KB, :] = jnp.zeros((KB, 2 * DH), BF16)
        c.wait()

        def turn(n, _):
            at = pl.ds(pl.multiple_of(n * KB, KB), KB)
            kt[:, at] = jnp.transpose(kv[at, 0:DH])
            return 0

        lax.fori_loop(0, kv.shape[0] // KB, turn, 0)

    for h in range(2 * heads):
        turned[h] = jnp.transpose(qg[:, h * DH : (h + 1) * DH])

    base = first[0] - lead
    q0 = lead + i * QB
    qrow = q0 + iota((1, QB), 1)
    drow = jnp.zeros((1, QB), jnp.int32)
    low = jnp.int32(0)
    high = jnp.int32(0)
    for start in starts_of(lengths):
        st = start - base
        low = jnp.where(st <= q0, st, low)
        high = jnp.where(st <= q0 + QB - 1, st, high)
        drow = jnp.where(st <= qrow, st, drow)
    end = q0 + QB
    blocks = (end - low + KB - 1) // KB
    begin = end - blocks * KB
    edge = blocks - 1
    full = jnp.minimum((high - begin + KB - 1) // KB, edge)
    scale = DH**-0.5 * LOG2E

    def fold(x):
        return x.reshape(-1, 8, QB)

    def place(b, n):
        return pl.ds(pl.multiple_of(KB + begin + b * KB + n * SUB, 128), SUB)

    def forward(masked, b, carry):
        new = []
        for h in range(heads):
            top, total, mean = carry[h]
            for n in range(KB // SUB):
                at = place(b, n)
                s = dot_nn(kv[at, 0:DH], turned[h])
                if masked:
                    key = begin + b * KB + n * SUB + iota((SUB, QB), 0)
                    s = jnp.where((key >= drow) & (key <= qrow), s, NEG)
                last = top
                top = jnp.maximum(top, jnp.max(jnp.max(fold(s), axis=0), axis=0, keepdims=True))
                e = jnp.exp2((s - top) * scale)
                gp = dot_nn(kv[at, DH : 2 * DH], turned[heads + h])
                part = slice(n * SUB, (n + 1) * SUB)
                e_scr[b, h, part, :] = e
                gp_scr[b, h, part, :] = gp
                tops[b, h, n] = jnp.broadcast_to(top, (8, QB))
                fade = jnp.exp2((last - top) * scale)
                total = total * fade + jnp.sum(fold(e), axis=0)
                mean = mean * fade + jnp.sum(fold(e * gp), axis=0)
            new.append((top, total, mean))
        return tuple(new)

    zero = jnp.zeros((8, QB), F32)
    carry = ((jnp.full((1, QB), NEG, F32), zero, zero),) * heads
    carry = lax.fori_loop(0, full, functools.partial(forward, True), carry)
    carry = lax.fori_loop(full, edge, functools.partial(forward, False), carry)
    carry = forward(True, edge, carry)
    peak = [c[0] for c in carry]
    total = [jnp.sum(c[1], axis=0, keepdims=True) for c in carry]
    centre = [jnp.sum(c[2], axis=0, keepdims=True) / t for c, t in zip(carry, total)]

    def grads(b, accs):
        new = []
        for h in range(heads):
            acc = accs[h]
            for n in range(KB // SUB):
                part = slice(n * SUB, (n + 1) * SUB)
                ds = (e_scr[b, h, part, :] * (gp_scr[b, h, part, :] - centre[h])).astype(BF16)
                fade = jnp.exp2((tops[b, h, n, 0:1, :] - peak[h]) * scale)
                acc += dot_nn(kt[:, place(b, n)], ds) * fade
            new.append(acc)
        return tuple(new)

    accs = lax.fori_loop(0, blocks, grads, (jnp.zeros((DH, QB), F32),) * heads)
    for h in range(heads):
        res = accs[h] * (DH**-0.5 / total[h])
        out[:, h * DH : (h + 1) * DH] = jnp.transpose(res).astype(BF16)


def attention(qg, kv, lengths, first):
    rows = qg.shape[0]
    heads = qg.shape[1] // (2 * DH)
    lead = REACH * rows
    most = (lead + QB - 1 + KB - 1) // KB
    return pl.pallas_call(
        attention_kernel,
        grid_spec=pltpu.PrefetchScalarGridSpec(
            num_scalar_prefetch=2,
            grid=(rows // QB,),
            in_specs=[
                pl.BlockSpec((QB, qg.shape[1]), lambda i, *_: (i, 0)),
                pl.BlockSpec(memory_space=pltpu.HBM),
            ],
            out_specs=pl.BlockSpec((QB, heads * DH), lambda i, *_: (i, 0)),
            scratch_shapes=[
                pltpu.VMEM((KB + lead + rows, 2 * DH), BF16),
                pltpu.VMEM((DH, KB + lead + rows), BF16),
                pltpu.VMEM((2 * heads, DH, QB), BF16),
                pltpu.VMEM((most, heads, KB, QB), F32),
                pltpu.VMEM((most, heads, KB, QB), F32),
                pltpu.VMEM((most, heads, KB // SUB, 8, QB), F32),
                pltpu.SemaphoreType.DMA((1,)),
            ],
        ),
        out_shape=jax.ShapeDtypeStruct((rows, heads * DH), BF16),
        compiler_params=pltpu.CompilerParams(vmem_limit_bytes=58 << 20),
        cost_estimate=pl.CostEstimate(flops=12 * 10**9, bytes_accessed=6 << 20, transcendentals=16 * 10**6),
        name="attention",
    )(lengths, first, qg, kv)


def split_sum(tri, dl):
    a = dl.astype(BF16)
    rest = dl - a.astype(F32)
    b = rest.astype(BF16)
    c = (rest - b.astype(F32)).astype(BF16)
    return dot_nn(tri, a) + dot_nn(tri, b) + dot_nn(tri, c)


def iota(shape, dim):
    return lax.broadcasted_iota(jnp.int32, shape, dim)


def starts_of(lengths):
    starts = [jnp.int32(0)]
    for j in range(lengths.shape[0] - 1):
        starts.append(starts[-1] + lengths[j])
    return starts


def rates_of(slow, fast, total_rows):
    rates = fast[...]
    lane = iota(rates.shape, 1)
    for n in range(slow.shape[0]):
        rates = jnp.where(lane == slow[n], 1.0 / total_rows, rates)
    return rates * -LOG2E


def doc_of(starts, pos):
    d = jnp.zeros(pos.shape, jnp.int32)
    for st in starts:
        d += (st <= pos).astype(jnp.int32)
    return d


def widen(values, spread):
    hi = values.astype(BF16)
    lo = (values - hi.astype(F32)).astype(BF16)
    return dot_nn(hi, spread) + dot_nn(lo, spread)


def edges(starts, first, c, st, rates):
    tri = (iota((BLOCK, BLOCK), 0) >= iota((BLOCK, BLOCK), 1)).astype(BF16)
    cum = split_sum(tri, st.astype(F32) * rates)
    begin = first + c * BLOCK
    doc_col = doc_of(starts, begin + iota((BLOCK, 1), 0))
    doc_last = doc_of(starts, begin + BLOCK - 1 + iota((1, 1), 0))
    doc_prev = doc_of(starts, begin - 1 + iota((1, 1), 0))
    total = cum[BLOCK - 1 : BLOCK, :]
    entering = jnp.exp2(jnp.where(doc_col == doc_prev, cum, NEG))
    to_end = jnp.exp2(jnp.where(doc_col == doc_last, total - cum, NEG))
    return cum, entering, to_end, doc_last == doc_prev


def spread_matrix(columns, group):
    return (iota((128, columns), 0) == group * (columns // HD) + iota((128, columns), 1) // HD).astype(BF16)


def edge_scratch(starts, first, st, rates, cum, cum_t, entering, to_end):
    @pl.when(pl.program_id(0) == 0)
    def _():
        a, b, c, _ = edges(starts, first[0], 0, st[...], rates[...])
        cum[...] = a
        cum_t[...] = jnp.transpose(a)
        entering[...] = b
        to_end[...] = c


MESH = pl.DeviceIdType.MESH


def links_of(rows):
    n = rows.shape[0] // 2
    return rows[0:n, :].astype(F32) + rows[n : 2 * n, :].astype(F32)


def first_kernel(
    lengths, slow, x, g, w, r, st, q, k, v, ag, fast,
    xs_out, gs_out, ws_out, rs_out, st_out, kv, qg, both,
    xs, gs, ws, rs, sts, ends_send, ends, lk, state, back, fs, fr, bs, br,
    own_sem, pair_send, pair_recv, head_send, head_recv, ends_ssem, ends_rsem, ring_ssem, ring_rsem, out_sem,
):
    ctx, hx, core = lax.axis_index("ctx"), lax.axis_index("hx"), lax.axis_index("core")
    slabs, chips, cores = lax.axis_size("ctx"), lax.axis_size("hx"), lax.axis_size("core")
    parts = chips * cores
    me = hx * cores + core
    other = 1 - core
    tokens = x.shape[0]
    rows = tokens * parts
    half = x.shape[1] // cores
    thin = w.shape[1] // cores
    qw = q.shape[1] // parts
    columns = half // chips
    heads = columns // HD
    begin = ctx * rows + hx * BLOCK
    starts = starts_of(lengths)

    def peer(d):
        p = lax.rem(me + d, parts)
        return p, {"hx": p // cores, "core": lax.rem(p, cores)}

    after = {"ctx": lax.rem(ctx + 1, slabs)}
    ahead = {"ctx": lax.rem(ctx + slabs - 1, slabs)}

    barrier = pltpu.get_barrier_semaphore()
    for d in range(1, parts):
        pl.semaphore_signal(barrier, inc=1, device_id=peer(d)[1], device_id_type=MESH)
    for n in (after, ahead):
        pl.semaphore_signal(barrier, inc=1, device_id=n, device_id_type=MESH)
    pl.semaphore_wait(barrier, parts + 1)

    def remote(src, dst, ssem, rsem, device):
        return pltpu.make_async_remote_copy(
            src_ref=src, dst_ref=dst, send_sem=ssem, recv_sem=rsem, device_id=device, device_id_type=MESH
        )

    def cols(n, width):
        return pl.ds(pl.multiple_of(n * width, 128), width)

    mine = pl.ds(pl.multiple_of(core * tokens, 128), tokens)
    pairs, owns = [], []
    for n, (src, dst, width) in enumerate(((x, xs, half), (g, gs, half), (w, ws, thin), (r, rs, thin), (st, sts, None))):
        theirs = src if width is None else src.at[:, cols(other, width)]
        ours = src if width is None else src.at[:, cols(core, width)]
        pairs.append(remote(theirs, dst.at[mine, :], pair_send.at[n], pair_recv.at[n], {"core": other}))
        owns.append(pltpu.make_async_copy(ours, dst.at[mine, :], own_sem.at[n]))
    for c in pairs + owns:
        c.start()
    lead = REACH * rows
    mine_kv = pl.ds(pl.multiple_of(lead + me * tokens, 128), tokens)
    mine_q = pl.ds(pl.multiple_of(me * tokens, 128), tokens)
    kv_moves, qg_moves, kv_own, qg_own = [], [], [], []
    for n, (src, dst, width, at, into, own) in enumerate(
        (
            (k, kv, DH, mine_kv, kv_moves, kv_own),
            (v, kv, DH, mine_kv, kv_moves, kv_own),
            (q, qg, qw, mine_q, qg_moves, qg_own),
            (ag, qg, qw, mine_q, qg_moves, qg_own),
        )
    ):
        place = slice((n % 2) * width, (n % 2 + 1) * width)
        for d in range(1, parts):
            p, device = peer(d)
            into.append(
                remote(src.at[:, cols(p, width)], dst.at[at, place], head_send.at[n, d], head_recv.at[n, d], device)
            )
        own.append(pltpu.make_async_copy(src.at[:, cols(me, width)], dst.at[at, place], own_sem.at[5 + n]))
    for c in kv_moves + kv_own + qg_own + qg_moves[:EARLY]:
        c.start()

    for c in owns:
        c.wait()
    for c in pairs:
        c.wait_recv()
    outs = [
        pltpu.make_async_copy(src, dst, out_sem.at[n])
        for n, (src, dst) in enumerate(((xs, xs_out), (gs, gs_out), (ws, ws_out), (rs, rs_out), (sts, st_out)))
    ]
    for c in outs:
        c.start()

    cum, entering, to_end, linked = edges(starts, begin, 0, sts[...], rates_of(slow, fast, rows * slabs))
    entering_hi = entering.astype(BF16)
    entering_lo = (entering - entering_hi.astype(F32)).astype(BF16)
    to_end_hi = to_end.astype(BF16)
    to_end_lo = (to_end - to_end_hi.astype(F32)).astype(BF16)
    tot = jnp.transpose(jnp.broadcast_to(cum[BLOCK - 1 : BLOCK, :], (128, 128)))
    link_all = jnp.exp2(jnp.where(linked, tot, NEG))

    def make_ends(group, out):
        spread = spread_matrix(columns, core * chips + group)
        wide_end = dot_nn(to_end_hi, spread) + dot_nn(to_end_lo, spread)
        wide_enter = dot_nn(entering_hi, spread) + dot_nn(entering_lo, spread)
        iw = (xs[:, cols(group, columns)].astype(F32) * wide_end).astype(BF16)
        gw = (gs[:, cols(group, columns)].astype(F32) * wide_enter).astype(BF16)
        out[0:columns, :] = dot_tn(iw, ws[:, cols(group, NS)]).astype(BF16)
        out[columns : 2 * columns, :] = dot_tn(gw, rs[:, cols(group, NS)]).astype(BF16)
        pick = (iota((heads, 128), 1) == (core * chips + group) * heads + iota((heads, 128), 0)).astype(F32)
        link = lax.dot_general(
            pick, link_all, (((1,), (0,)), ((), ())), precision=lax.Precision.HIGHEST, preferred_element_type=F32
        )
        hi = link.astype(BF16)
        out[2 * columns : 2 * columns + heads, :] = hi
        out[2 * columns + heads : 2 * columns + 2 * heads, :] = (link - hi.astype(F32)).astype(BF16)

    hops = []
    for n in range(REACH):
        src = pl.ds((REACH - n) * rows, rows)
        dst = pl.ds((REACH - n - 1) * rows, rows)
        hops.append(remote(kv.at[src, :], kv.at[dst, :], ring_ssem.at[n], ring_rsem.at[n], after))

    end_moves = []
    for d in range(1, chips):
        to = lax.rem(hx + d, chips)
        make_ends(to, ends_send.at[d - 1])
        c = remote(ends_send.at[d - 1], ends.at[hx], ends_ssem.at[d], ends_rsem.at[d], {"hx": to})
        c.start()
        end_moves.append(c)
        if d == 2:
            for c in kv_own:
                c.wait()
            for c in kv_moves:
                c.wait_recv()
            hops[0].start()
    make_ends(hx, ends.at[hx])

    hops[0].wait_recv()
    hops[1].start()

    for c in end_moves:
        c.wait_recv()
    for c in qg_moves[EARLY:]:
        c.start()
    for n in range(chips):
        lk[n] = links_of(ends[n, 2 * columns :, :])
    prods = [None, lk[0]]
    for n in range(1, chips):
        prods.append(prods[-1] * lk[n])
    for n in range(1, chips + 1):
        lk[chips + n - 1] = prods[n]
    whole = 2 * chips - 1

    def head_rows(h):
        return pl.ds(pl.multiple_of(h * HD, HD), HD), pl.ds(pl.multiple_of(columns + h * HD, HD), HD)

    def totals(h, _):
        at, bt = head_rows(h)
        one = pl.ds(h, 1)
        s = ends[0, at, :].astype(F32)
        b = ends[0, bt, :].astype(F32)
        for n in range(1, chips):
            s = lk[n, one, :] * s + ends[n, at, :].astype(F32)
            b = b + lk[chips + n - 1, one, :] * ends[n, bt, :].astype(F32)
        state[at, :] = s
        back[at, :] = b
        fs[0, at, :] = s.astype(BF16)
        bs[0, at, :] = b.astype(BF16)
        return 0

    def ring(src, dst, sem, device):
        moves = []
        for n in range(REACH):
            pair = []
            for part in range(2):
                at = pl.ds(part * columns // 2, columns // 2)
                k = sem + 2 * n + part
                pair.append(remote(src.at[n, at, :], dst.at[n, at, :], ring_ssem.at[k], ring_rsem.at[k], device))
            moves.append(pair)
        return moves

    fwd = ring(fs, fr, REACH, after)
    bwd = ring(bs, br, 3 * REACH, ahead)

    def over(part, body):
        lax.fori_loop(part * heads // 2, (part + 1) * heads // 2, body, 0)

    for part in range(2):
        over(part, totals)
        fwd[0][part].start()
        bwd[0][part].start()
    hops[1].wait_recv()
    hops[2].start()
    for n in range(1, REACH):
        for part in range(2):
            for moves, base, recv, send in ((bwd, back, br, bs), (fwd, state, fr, fs)):
                moves[n - 1][part].wait_recv()

                def step(h, _):
                    at, unused = head_rows(h)
                    val = base[at, :] + lk[whole, pl.ds(h, 1), :] * recv[n - 1, at, :].astype(F32)
                    send[n, at, :] = val.astype(BF16)
                    return 0

                over(part, step)
                moves[n][part].start()

    def chip_states(h, _):
        at, bt = head_rows(h)
        one = pl.ds(h, 1)
        s = fr[REACH - 1, at, :].astype(F32)
        b = br[REACH - 1, at, :].astype(F32)
        for n in range(chips):
            both[n, at, :] = s.astype(BF16)
            s = lk[n, one, :] * s + ends[n, at, :].astype(F32)
        for n in reversed(range(chips)):
            both[n, bt, :] = b.astype(BF16)
            b = lk[n, one, :] * b + ends[n, bt, :].astype(F32)
        return 0

    for part in range(2):
        bwd[REACH - 1][part].wait_recv()
        fwd[REACH - 1][part].wait_recv()
        over(part, chip_states)
    hops[REACH - 1].wait_recv()
    for c in qg_own + outs:
        c.wait()
    for c in qg_moves:
        c.wait_recv()
    for c in pairs + kv_moves + qg_moves + end_moves + hops + sum(fwd + bwd, []):
        c.wait_send()


def first_stage(lengths, slow, x, g, w, r, st, q, k, v, ag, fast, parts, cores):
    chips = parts // cores
    tokens = x.shape[0]
    rows = tokens * parts
    half, thin = x.shape[1] // cores, w.shape[1] // cores
    columns = half // chips
    heads = columns // HD
    packed = 2 * columns + 2 * heads
    both_rows = cores * tokens
    hbm = pl.BlockSpec(memory_space=pltpu.HBM)
    vmem = pl.BlockSpec(memory_space=pltpu.VMEM)
    dma = pltpu.SemaphoreType.DMA
    return pl.pallas_call(
        first_kernel,
        in_specs=[pl.BlockSpec(memory_space=pltpu.SMEM)] * 2 + [hbm] * 9 + [vmem],
        out_specs=[hbm] * 7 + [vmem],
        out_shape=[
            jax.ShapeDtypeStruct((both_rows, half), BF16),
            jax.ShapeDtypeStruct((both_rows, half), BF16),
            jax.ShapeDtypeStruct((both_rows, thin), BF16),
            jax.ShapeDtypeStruct((both_rows, thin), BF16),
            jax.ShapeDtypeStruct((both_rows, st.shape[1]), BF16),
            jax.ShapeDtypeStruct(((REACH + 1) * rows, 2 * DH), BF16),
            jax.ShapeDtypeStruct((rows, 2 * q.shape[1] // parts), BF16),
            jax.ShapeDtypeStruct((chips, 2 * columns, NS), BF16),
        ],
        scratch_shapes=[
            pltpu.VMEM((both_rows, half), BF16),
            pltpu.VMEM((both_rows, half), BF16),
            pltpu.VMEM((both_rows, thin), BF16),
            pltpu.VMEM((both_rows, thin), BF16),
            pltpu.VMEM((both_rows, st.shape[1]), BF16),
            pltpu.VMEM((chips - 1, packed, NS), BF16),
            pltpu.VMEM((chips, packed, NS), BF16),
            pltpu.VMEM((2 * chips, heads, 128), F32),
            pltpu.VMEM((columns, NS), F32),
            pltpu.VMEM((columns, NS), F32),
            pltpu.VMEM((REACH, columns, NS), BF16),
            pltpu.VMEM((REACH, columns, NS), BF16),
            pltpu.VMEM((REACH, columns, NS), BF16),
            pltpu.VMEM((REACH, columns, NS), BF16),
            dma((9,)),
            dma((5,)),
            dma((5,)),
            dma((4, parts)),
            dma((4, parts)),
            dma((chips,)),
            dma((chips,)),
            dma((REACH * 5,)),
            dma((REACH * 5,)),
            dma((5,)),
        ],
        compiler_params=pltpu.CompilerParams(vmem_limit_bytes=60 << 20, collective_id=0, has_side_effects=True),
        cost_estimate=pl.CostEstimate(flops=2 * 10**9, bytes_accessed=16 << 20, transcendentals=10**5),
        name="first_stage",
    )(lengths, slow, x, g, w, r, st, q, k, v, ag, fast)


EDGES = [
    pltpu.VMEM((BLOCK, 128), F32),
    pltpu.VMEM((128, BLOCK), F32),
    pltpu.VMEM((BLOCK, 128), F32),
    pltpu.VMEM((BLOCK, 128), F32),
]


def last_kernel(
    lengths, slow, x, g, w, r, st, fast, gains, both, grad_q, out_x, out_w, out_r, out_q,
    cum, cum_t, entering, to_end, res_x, res_w, res_r, own_sem, pair_send, pair_recv, q_send, q_recv,
):
    j = pl.program_id(0)
    ctx, hx, core = lax.axis_index("ctx"), lax.axis_index("hx"), lax.axis_index("core")
    chips, cores = lax.axis_size("hx"), lax.axis_size("core")
    parts = chips * cores
    me = hx * cores + core
    other = 1 - core
    tokens = out_x.shape[0]
    columns = x.shape[1]
    heads = columns // HD
    qw = grad_q.shape[1]
    begin = ctx * tokens * parts + hx * BLOCK
    group = core * chips + j
    starts = starts_of(lengths)

    def cols(n, width):
        return pl.ds(pl.multiple_of(n * width, 128), width)

    def remote(src, dst, ssem, rsem, device):
        return pltpu.make_async_remote_copy(
            src_ref=src, dst_ref=dst, send_sem=ssem, recv_sem=rsem, device_id=device, device_id_type=MESH
        )

    def q_moves():
        moves = []
        for d in range(1, parts):
            p = lax.rem(me + d, parts)
            device = {"hx": p // cores, "core": lax.rem(p, cores)}
            moves.append(remote(grad_q.at[cols(p, tokens), :], out_q.at[:, cols(me, qw)], q_send.at[d], q_recv.at[d], device))
        own = pltpu.make_async_copy(grad_q.at[cols(me, tokens), :], out_q.at[:, cols(me, qw)], own_sem.at[chips, 0])
        return moves, own

    def pair_moves(n):
        moves, owns = [], []
        for k, (res, out, width) in enumerate(((res_x, out_x, columns), (res_w, out_w, NS), (res_r, out_r, NS))):
            place = out.at[:, cols(core * chips + n, width)]
            moves.append(
                remote(res.at[n, cols(other, tokens), :], place, pair_send.at[n, k], pair_recv.at[n, k], {"core": other})
            )
            owns.append(pltpu.make_async_copy(res.at[n, cols(core, tokens), :], place, own_sem.at[n, k]))
        return moves, owns

    @pl.when(j == 0)
    def _():
        barrier = pltpu.get_barrier_semaphore()
        for d in range(1, parts):
            p = lax.rem(me + d, parts)
            pl.semaphore_signal(
                barrier, inc=1, device_id={"hx": p // cores, "core": lax.rem(p, cores)}, device_id_type=MESH
            )
        pl.semaphore_wait(barrier, parts - 1)
        moves, own = q_moves()
        for c in moves + [own]:
            c.start()
        a, b, c, _ = edges(starts, begin, 0, st[...], rates_of(slow, fast, tokens * parts * lax.axis_size("ctx")))
        cum[...] = a
        cum_t[...] = jnp.transpose(a)
        entering[...] = b
        to_end[...] = c

    doc_col = doc_of(starts, begin + iota((BLOCK, 1), 0))
    doc_row = doc_of(starts, begin + iota((1, BLOCK), 1))
    ok = (iota((BLOCK, BLOCK), 0) <= iota((BLOCK, BLOCK), 1)) & (doc_col == doc_row)
    spread = spread_matrix(columns, group)
    skips = widen(jnp.broadcast_to(gains[...], (8, 128)), spread)[0:1, :]
    end_wide = widen(to_end[...], spread)
    iw = (x[...].astype(F32) * end_wide).astype(BF16)
    gw = (g[...].astype(F32) * widen(entering[...], spread)).astype(BF16)
    wv = w[...]
    rv = r[...]
    state = both[0, 0:columns, :]
    back = both[0, columns : 2 * columns, :]
    carried = dot_nt(wv, back)
    scores = dot_nt(wv, rv)
    joint = jnp.zeros((BLOCK, BLOCK), F32)
    lane = iota((BLOCK, 2 * HD), 1) < HD
    offset = pl.multiple_of(group * heads, heads)
    rows_t = cum_t[pl.ds(offset, heads), :]
    cols_all = jnp.transpose(jnp.concatenate([rows_t, jnp.zeros((128 - heads, BLOCK), F32)], axis=0))
    for p in range(heads // 2):
        at = slice(p * 2 * HD, (p + 1) * 2 * HD)
        xp = x[:, at]
        gp = g[:, at]
        zero = jnp.zeros_like(xp)
        inner = skips[:, at] * gp.astype(F32) + end_wide[:, at] * carried[:, at]
        for half in range(2):
            h = 2 * p + half
            mine = lane if half == 0 else ~lane
            decay = jnp.exp2(jnp.where(ok, rows_t[h : h + 1, :] - cols_all[:, h : h + 1], NEG))
            joint += decay * dot_nt(jnp.where(mine, xp, zero), gp)
            mixing = (scores * decay).astype(BF16)
            inner += dot_nn(mixing, jnp.where(mine, gp, zero))
        res_x[j, :, at] = inner.astype(BF16)
    low = joint.astype(BF16)
    res_w[j] = (dot_nn(low, rv) + dot_nn(iw, back)).astype(BF16)
    res_r[j] = (dot_tn(low, wv) + dot_nn(gw, state)).astype(BF16)

    for n in range(chips):

        @pl.when(j == n)
        def _():
            moves, owns = pair_moves(n)
            for c in moves + owns:
                c.start()

    @pl.when(j == chips - 1)
    def _():
        moves, own = q_moves()
        own.wait()
        for c in moves:
            c.wait_recv()
        for c in moves:
            c.wait_send()
        for n in range(chips):
            moves, owns = pair_moves(n)
            for c in owns:
                c.wait()
            for c in moves:
                c.wait_recv()
            for c in moves:
                c.wait_send()


def last_stage(lengths, slow, mix, fast, gains, both, grad_q, parts, cores):
    chips = both.shape[0]
    columns = both.shape[1] // 2
    tokens = BLOCK // cores
    groups = chips * cores
    hbm = pl.BlockSpec(memory_space=pltpu.HBM)
    dma = pltpu.SemaphoreType.DMA
    return pl.pallas_call(
        last_kernel,
        grid_spec=pltpu.PrefetchScalarGridSpec(
            num_scalar_prefetch=2,
            grid=(chips,),
            in_specs=[
                pl.BlockSpec((BLOCK, columns), lambda j, *_: (0, j)),
                pl.BlockSpec((BLOCK, columns), lambda j, *_: (0, j)),
                pl.BlockSpec((BLOCK, NS), lambda j, *_: (0, j)),
                pl.BlockSpec((BLOCK, NS), lambda j, *_: (0, j)),
                pl.BlockSpec((BLOCK, 128), lambda j, *_: (0, 0)),
                pl.BlockSpec((1, 128), lambda j, *_: (0, 0)),
                pl.BlockSpec((1, 128), lambda j, *_: (0, 0)),
                pl.BlockSpec((1, 2 * columns, NS), lambda j, *_: (j, 0, 0)),
                hbm,
            ],
            out_specs=[hbm] * 4,
            scratch_shapes=EDGES
            + [
                pltpu.VMEM((chips, BLOCK, columns), BF16),
                pltpu.VMEM((chips, BLOCK, NS), BF16),
                pltpu.VMEM((chips, BLOCK, NS), BF16),
                dma((chips + 1, 3)),
                dma((chips, 3)),
                dma((chips, 3)),
                dma((parts,)),
                dma((parts,)),
            ],
        ),
        out_shape=[
            jax.ShapeDtypeStruct((tokens, groups * columns), BF16),
            jax.ShapeDtypeStruct((tokens, groups * NS), BF16),
            jax.ShapeDtypeStruct((tokens, groups * NS), BF16),
            jax.ShapeDtypeStruct((tokens, parts * grad_q.shape[1]), BF16),
        ],
        compiler_params=pltpu.CompilerParams(vmem_limit_bytes=56 << 20, collective_id=1, has_side_effects=True),
        cost_estimate=pl.CostEstimate(flops=8 * 10**9, bytes_accessed=14 << 20, transcendentals=5 * 10**6),
        name="last_stage",
    )(lengths, slow, *mix, fast, gains, both, grad_q)


HEAD = ("hx", "core")


def shards(x, w, r, steps, fast_rates, slow_heads, skip_gains, grad, q, k, v, ag, doc_lengths):
    parts = lax.axis_size(HEAD)
    cores = lax.axis_size("core")
    slab_first = (lax.axis_index("ctx") * x.shape[0] * parts).astype(jnp.int32).reshape(1)
    fast = fast_rates.reshape(1, MH)
    gains = skip_gains.reshape(1, MH)
    *mix, kv, qg, both = first_stage(doc_lengths, slow_heads, x, grad, w, r, steps, q, k, v, ag, fast, parts, cores)
    both = lax.all_to_all(both, "hx", split_axis=0, concat_axis=0, tiled=True)
    grad_q = attention(qg, kv, doc_lengths, slab_first)
    return tuple(last_stage(doc_lengths, slow_heads, mix, fast, gains, both, grad_q, parts, cores))


def solution(mesh):
    split = Mesh(mesh.devices.reshape(mesh.shape["ctx"], -1, 2), ("ctx", "hx", "core"))
    tokens = P(("ctx", "hx", "core"), None)
    return jax.shard_map(
        shards,
        mesh=split,
        in_specs=(tokens, tokens, tokens, tokens, P(), P(), P(), tokens, tokens, tokens, tokens, tokens, P()),
        out_specs=(tokens, tokens, tokens, tokens),
        check_vma=False,
    )
```

```python
import functools

import jax
import jax.numpy as jnp
from jax import lax
from jax.experimental import pallas as pl
from jax.experimental.pallas import tpu as pltpu
from jax.sharding import Mesh
from jax.sharding import PartitionSpec as P

MH = 128
HD = 64
NS = 128
DH = 128
BLOCK = 256
LOG2E = 1.4426950408889634
REACH = 3
QB = 256
KB = 512
SUB = 256
EARLY = 3
NEG = -1e30

F32 = jnp.float32
BF16 = jnp.bfloat16


def dot_nt(a, b):
    return lax.dot_general(a, b, (((1,), (1,)), ((), ())), preferred_element_type=F32)


def dot_nn(a, b):
    return lax.dot_general(a, b, (((1,), (0,)), ((), ())), preferred_element_type=F32)


def dot_tn(a, b):
    return lax.dot_general(a, b, (((0,), (0,)), ((), ())), preferred_element_type=F32)


def attention_kernel(lengths, first, qg, kv_all, out, kv, kt, turned, e_scr, gp_scr, tops, sems):
    i = pl.program_id(0)
    rows = kv_all.shape[0] // (REACH + 1)
    lead = REACH * rows
    heads = out.shape[1] // DH

    @pl.when(i == 0)
    def _():
        c = pltpu.make_async_copy(kv_all, kv.at[pl.ds(KB, kv_all.shape[0]), :], sems.at[0])
        c.start()
        kv[0:KB, :] = jnp.zeros((KB, 2 * DH), BF16)
        c.wait()

        def turn(n, _):
            at = pl.ds(pl.multiple_of(n * KB, KB), KB)
            kt[:, at] = jnp.transpose(kv[at, 0:DH])
            return 0

        lax.fori_loop(0, kv.shape[0] // KB, turn, 0)

    for h in range(2 * heads):
        turned[h] = jnp.transpose(qg[:, h * DH : (h + 1) * DH])

    base = first[0] - lead
    q0 = lead + i * QB
    qrow = q0 + iota((1, QB), 1)
    drow = jnp.zeros((1, QB), jnp.int32)
    low = jnp.int32(0)
    high = jnp.int32(0)
    for start in starts_of(lengths):
        st = start - base
        low = jnp.where(st <= q0, st, low)
        high = jnp.where(st <= q0 + QB - 1, st, high)
        drow = jnp.where(st <= qrow, st, drow)
    end = q0 + QB
    blocks = (end - low + KB - 1) // KB
    begin = end - blocks * KB
    edge = blocks - 1
    full = jnp.minimum((high - begin + KB - 1) // KB, edge)
    scale = DH**-0.5 * LOG2E

    def fold(x):
        return x.reshape(-1, 8, QB)

    def place(b, n):
        return pl.ds(pl.multiple_of(KB + begin + b * KB + n * SUB, 128), SUB)

    def forward(masked, b, carry):
        new = []
        for h in range(heads):
            top, total, mean = carry[h]
            for n in range(KB // SUB):
                at = place(b, n)
                s = dot_nn(kv[at, 0:DH], turned[h])
                if masked:
                    key = begin + b * KB + n * SUB + iota((SUB, QB), 0)
                    s = jnp.where((key >= drow) & (key <= qrow), s, NEG)
                last = top
                top = jnp.maximum(top, jnp.max(jnp.max(fold(s), axis=0), axis=0, keepdims=True))
                e = jnp.exp2((s - top) * scale)
                gp = dot_nn(kv[at, DH : 2 * DH], turned[heads + h])
                part = slice(n * SUB, (n + 1) * SUB)
                e_scr[b, h, part, :] = e
                gp_scr[b, h, part, :] = gp
                tops[b, h, n] = jnp.broadcast_to(top, (8, QB))
                fade = jnp.exp2((last - top) * scale)
                total = total * fade + jnp.sum(fold(e), axis=0)
                mean = mean * fade + jnp.sum(fold(e * gp), axis=0)
            new.append((top, total, mean))
        return tuple(new)

    zero = jnp.zeros((8, QB), F32)
    carry = ((jnp.full((1, QB), NEG, F32), zero, zero),) * heads
    carry = lax.fori_loop(0, full, functools.partial(forward, True), carry)
    carry = lax.fori_loop(full, edge, functools.partial(forward, False), carry)
    carry = forward(True, edge, carry)
    peak = [c[0] for c in carry]
    total = [jnp.sum(c[1], axis=0, keepdims=True) for c in carry]
    centre = [jnp.sum(c[2], axis=0, keepdims=True) / t for c, t in zip(carry, total)]

    def grads(b, accs):
        new = []
        for h in range(heads):
            acc = accs[h]
            for n in range(KB // SUB):
                part = slice(n * SUB, (n + 1) * SUB)
                ds = (e_scr[b, h, part, :] * (gp_scr[b, h, part, :] - centre[h])).astype(BF16)
                fade = jnp.exp2((tops[b, h, n, 0:1, :] - peak[h]) * scale)
                acc += dot_nn(kt[:, place(b, n)], ds) * fade
            new.append(acc)
        return tuple(new)

    accs = lax.fori_loop(0, blocks, grads, (jnp.zeros((DH, QB), F32),) * heads)
    for h in range(heads):
        res = accs[h] * (DH**-0.5 / total[h])
        out[:, h * DH : (h + 1) * DH] = jnp.transpose(res).astype(BF16)


def attention(qg, kv, lengths, first):
    rows = qg.shape[0]
    heads = qg.shape[1] // (2 * DH)
    lead = REACH * rows
    most = (lead + QB - 1 + KB - 1) // KB
    return pl.pallas_call(
        attention_kernel,
        grid_spec=pltpu.PrefetchScalarGridSpec(
            num_scalar_prefetch=2,
            grid=(rows // QB,),
            in_specs=[
                pl.BlockSpec((QB, qg.shape[1]), lambda i, *_: (i, 0)),
                pl.BlockSpec(memory_space=pltpu.HBM),
            ],
            out_specs=pl.BlockSpec((QB, heads * DH), lambda i, *_: (i, 0)),
            scratch_shapes=[
                pltpu.VMEM((KB + lead + rows, 2 * DH), BF16),
                pltpu.VMEM((DH, KB + lead + rows), BF16),
                pltpu.VMEM((2 * heads, DH, QB), BF16),
                pltpu.VMEM((most, heads, KB, QB), F32),
                pltpu.VMEM((most, heads, KB, QB), F32),
                pltpu.VMEM((most, heads, KB // SUB, 8, QB), F32),
                pltpu.SemaphoreType.DMA((1,)),
            ],
        ),
        out_shape=jax.ShapeDtypeStruct((rows, heads * DH), BF16),
        compiler_params=pltpu.CompilerParams(vmem_limit_bytes=58 << 20),
        cost_estimate=pl.CostEstimate(flops=12 * 10**9, bytes_accessed=6 << 20, transcendentals=16 * 10**6),
        name="attention",
    )(lengths, first, qg, kv)


def split_sum(tri, dl):
    a = dl.astype(BF16)
    rest = dl - a.astype(F32)
    b = rest.astype(BF16)
    c = (rest - b.astype(F32)).astype(BF16)
    return dot_nn(tri, a) + dot_nn(tri, b) + dot_nn(tri, c)


def iota(shape, dim):
    return lax.broadcasted_iota(jnp.int32, shape, dim)


def starts_of(lengths):
    starts = [jnp.int32(0)]
    for j in range(lengths.shape[0] - 1):
        starts.append(starts[-1] + lengths[j])
    return starts


def rates_of(slow, fast, total_rows):
    rates = fast[...]
    lane = iota(rates.shape, 1)
    for n in range(slow.shape[0]):
        rates = jnp.where(lane == slow[n], 1.0 / total_rows, rates)
    return rates * -LOG2E


def doc_of(starts, pos):
    d = jnp.zeros(pos.shape, jnp.int32)
    for st in starts:
        d += (st <= pos).astype(jnp.int32)
    return d


def widen(values, spread):
    hi = values.astype(BF16)
    lo = (values - hi.astype(F32)).astype(BF16)
    return dot_nn(hi, spread) + dot_nn(lo, spread)


def edges(starts, first, c, st, rates):
    tri = (iota((BLOCK, BLOCK), 0) >= iota((BLOCK, BLOCK), 1)).astype(BF16)
    cum = split_sum(tri, st.astype(F32) * rates)
    begin = first + c * BLOCK
    doc_col = doc_of(starts, begin + iota((BLOCK, 1), 0))
    doc_last = doc_of(starts, begin + BLOCK - 1 + iota((1, 1), 0))
    doc_prev = doc_of(starts, begin - 1 + iota((1, 1), 0))
    total = cum[BLOCK - 1 : BLOCK, :]
    entering = jnp.exp2(jnp.where(doc_col == doc_prev, cum, NEG))
    to_end = jnp.exp2(jnp.where(doc_col == doc_last, total - cum, NEG))
    return cum, entering, to_end, doc_last == doc_prev


def spread_matrix(columns, group):
    return (iota((128, columns), 0) == group * (columns // HD) + iota((128, columns), 1) // HD).astype(BF16)


MESH = pl.DeviceIdType.MESH


def links_of(rows):
    n = rows.shape[0] // 2
    return rows[0:n, :].astype(F32) + rows[n : 2 * n, :].astype(F32)


def first_kernel(
    lengths, slow, x, g, w, r, st, q, k, v, ag, fast, gains,
    xs_out, gs_out, ws_out, st_out, ix_out, iw_out, ir_out, kv, qg, both,
    xs, gs, ws, rs, sts, ix, iw_in, ir_in, cum_t, ends_send, ends, lk, state, back, fs, fr, bs, br,
    own_sem, pair_send, pair_recv, head_send, head_recv, ends_ssem, ends_rsem, ring_ssem, ring_rsem, out_sem,
):
    ctx, hx, core = lax.axis_index("ctx"), lax.axis_index("hx"), lax.axis_index("core")
    slabs, chips, cores = lax.axis_size("ctx"), lax.axis_size("hx"), lax.axis_size("core")
    parts = chips * cores
    me = hx * cores + core
    other = 1 - core
    tokens = x.shape[0]
    rows = tokens * parts
    half = x.shape[1] // cores
    thin = w.shape[1] // cores
    qw = q.shape[1] // parts
    columns = half // chips
    heads = columns // HD
    begin = ctx * rows + hx * BLOCK
    starts = starts_of(lengths)

    def peer(d):
        p = lax.rem(me + d, parts)
        return p, {"hx": p // cores, "core": lax.rem(p, cores)}

    after = {"ctx": lax.rem(ctx + 1, slabs)}
    ahead = {"ctx": lax.rem(ctx + slabs - 1, slabs)}

    barrier = pltpu.get_barrier_semaphore()
    for d in range(1, parts):
        pl.semaphore_signal(barrier, inc=1, device_id=peer(d)[1], device_id_type=MESH)
    for n in (after, ahead):
        pl.semaphore_signal(barrier, inc=1, device_id=n, device_id_type=MESH)
    pl.semaphore_wait(barrier, parts + 1)

    def remote(src, dst, ssem, rsem, device):
        return pltpu.make_async_remote_copy(
            src_ref=src, dst_ref=dst, send_sem=ssem, recv_sem=rsem, device_id=device, device_id_type=MESH
        )

    def cols(n, width):
        return pl.ds(pl.multiple_of(n * width, 128), width)

    mine = pl.ds(pl.multiple_of(core * tokens, 128), tokens)
    pairs, owns = [], []
    for n, (src, dst, width) in enumerate(((x, xs, half), (g, gs, half), (w, ws, thin), (r, rs, thin), (st, sts, None))):
        theirs = src if width is None else src.at[:, cols(other, width)]
        ours = src if width is None else src.at[:, cols(core, width)]
        pairs.append(remote(theirs, dst.at[mine, :], pair_send.at[n], pair_recv.at[n], {"core": other}))
        owns.append(pltpu.make_async_copy(ours, dst.at[mine, :], own_sem.at[n]))
    for c in pairs + owns:
        c.start()
    lead = REACH * rows
    mine_kv = pl.ds(pl.multiple_of(lead + me * tokens, 128), tokens)
    mine_q = pl.ds(pl.multiple_of(me * tokens, 128), tokens)
    kv_moves, qg_moves, kv_own, qg_own = [], [], [], []
    for n, (src, dst, width, at, into, own) in enumerate(
        (
            (k, kv, DH, mine_kv, kv_moves, kv_own),
            (v, kv, DH, mine_kv, kv_moves, kv_own),
            (q, qg, qw, mine_q, qg_moves, qg_own),
            (ag, qg, qw, mine_q, qg_moves, qg_own),
        )
    ):
        place = slice((n % 2) * width, (n % 2 + 1) * width)
        for d in range(1, parts):
            p, device = peer(d)
            into.append(
                remote(src.at[:, cols(p, width)], dst.at[at, place], head_send.at[n, d], head_recv.at[n, d], device)
            )
        own.append(pltpu.make_async_copy(src.at[:, cols(me, width)], dst.at[at, place], own_sem.at[5 + n]))
    for c in kv_moves + kv_own + qg_own + qg_moves[:EARLY]:
        c.start()

    for c in owns:
        c.wait()
    for c in pairs:
        c.wait_recv()
    outs = [
        pltpu.make_async_copy(src, dst, out_sem.at[n])
        for n, (src, dst) in enumerate(((xs, xs_out), (gs, gs_out), (ws, ws_out), (sts, st_out)))
    ]
    for c in outs:
        c.start()

    cum, entering, to_end, linked = edges(starts, begin, 0, sts[...], rates_of(slow, fast, rows * slabs))
    entering_hi = entering.astype(BF16)
    entering_lo = (entering - entering_hi.astype(F32)).astype(BF16)
    to_end_hi = to_end.astype(BF16)
    to_end_lo = (to_end - to_end_hi.astype(F32)).astype(BF16)
    tot = jnp.transpose(jnp.broadcast_to(cum[BLOCK - 1 : BLOCK, :], (128, 128)))
    link_all = jnp.exp2(jnp.where(linked, tot, NEG))

    def make_ends(group, out):
        spread = spread_matrix(columns, core * chips + group)
        wide_end = dot_nn(to_end_hi, spread) + dot_nn(to_end_lo, spread)
        wide_enter = dot_nn(entering_hi, spread) + dot_nn(entering_lo, spread)
        iw = (xs[:, cols(group, columns)].astype(F32) * wide_end).astype(BF16)
        gw = (gs[:, cols(group, columns)].astype(F32) * wide_enter).astype(BF16)
        out[0:columns, :] = dot_tn(iw, ws[:, cols(group, NS)]).astype(BF16)
        out[columns : 2 * columns, :] = dot_tn(gw, rs[:, cols(group, NS)]).astype(BF16)
        pick = (iota((heads, 128), 1) == (core * chips + group) * heads + iota((heads, 128), 0)).astype(F32)
        link = lax.dot_general(
            pick, link_all, (((1,), (0,)), ((), ())), precision=lax.Precision.HIGHEST, preferred_element_type=F32
        )
        hi = link.astype(BF16)
        out[2 * columns : 2 * columns + heads, :] = hi
        out[2 * columns + heads : 2 * columns + 2 * heads, :] = (link - hi.astype(F32)).astype(BF16)

    hops = []
    for n in range(REACH):
        src = pl.ds((REACH - n) * rows, rows)
        dst = pl.ds((REACH - n - 1) * rows, rows)
        hops.append(remote(kv.at[src, :], kv.at[dst, :], ring_ssem.at[n], ring_rsem.at[n], after))

    end_moves = []
    for d in range(1, chips):
        to = lax.rem(hx + d, chips)
        make_ends(to, ends_send.at[d - 1])
        c = remote(ends_send.at[d - 1], ends.at[hx], ends_ssem.at[d], ends_rsem.at[d], {"hx": to})
        c.start()
        end_moves.append(c)
        if d == 2:
            for c in kv_own:
                c.wait()
            for c in kv_moves:
                c.wait_recv()
            hops[0].start()
    make_ends(hx, ends.at[hx])

    cum_t[...] = jnp.transpose(cum)
    doc_col = doc_of(starts, begin + iota((BLOCK, 1), 0))
    doc_row = doc_of(starts, begin + iota((1, BLOCK), 1))
    ok = (iota((BLOCK, BLOCK), 0) <= iota((BLOCK, BLOCK), 1)) & (doc_col == doc_row)
    lane = iota((BLOCK, 2 * HD), 1) < HD

    def inside(group, _):
        spread = spread_matrix(columns, core * chips + group)
        skips = widen(jnp.broadcast_to(gains[...], (8, 128)), spread)[0:1, :]
        wv = ws[:, cols(group, NS)]
        rv = rs[:, cols(group, NS)]
        scores = dot_nt(wv, rv)
        joint = jnp.zeros((BLOCK, BLOCK), F32)
        offset = pl.multiple_of((core * chips + group) * heads, heads)
        rows_t = cum_t[pl.ds(offset, heads), :]
        cols_t = jnp.transpose(jnp.concatenate([rows_t, jnp.zeros((128 - heads, BLOCK), F32)], axis=0))
        for p in range(heads // 2):
            at = pl.ds(pl.multiple_of(group * columns + p * 2 * HD, 2 * HD), 2 * HD)
            xp = xs[:, at]
            gp = gs[:, at]
            zero = jnp.zeros_like(xp)
            inner = skips[:, p * 2 * HD : (p + 1) * 2 * HD] * gp.astype(F32)
            for part in range(2):
                h = 2 * p + part
                mine = lane if part == 0 else ~lane
                decay = jnp.exp2(jnp.where(ok, rows_t[h : h + 1, :] - cols_t[:, h : h + 1], NEG))
                joint += decay * dot_nt(jnp.where(mine, xp, zero), gp)
                mixing = (scores * decay).astype(BF16)
                inner += dot_nn(mixing, jnp.where(mine, gp, zero))
            ix[:, at] = inner
        low = joint.astype(BF16)
        iw_in[:, cols(group, NS)] = dot_nn(low, rv)
        ir_in[:, cols(group, NS)] = dot_tn(low, wv)
        return 0

    lax.fori_loop(0, chips // 2, inside, 0)
    hops[0].wait_recv()
    hops[1].start()
    lax.fori_loop(chips // 2, chips, inside, 0)
    more = [
        pltpu.make_async_copy(src, dst, out_sem.at[4 + n])
        for n, (src, dst) in enumerate(((ix, ix_out), (iw_in, iw_out), (ir_in, ir_out)))
    ]
    for c in more:
        c.start()

    for c in end_moves:
        c.wait_recv()
    for c in qg_moves[EARLY:]:
        c.start()
    for n in range(chips):
        lk[n] = links_of(ends[n, 2 * columns :, :])
    prods = [None, lk[0]]
    for n in range(1, chips):
        prods.append(prods[-1] * lk[n])
    for n in range(1, chips + 1):
        lk[chips + n - 1] = prods[n]
    whole = 2 * chips - 1

    def head_rows(h):
        return pl.ds(pl.multiple_of(h * HD, HD), HD), pl.ds(pl.multiple_of(columns + h * HD, HD), HD)

    def totals(h, _):
        at, bt = head_rows(h)
        one = pl.ds(h, 1)
        s = ends[0, at, :].astype(F32)
        b = ends[0, bt, :].astype(F32)
        for n in range(1, chips):
            s = lk[n, one, :] * s + ends[n, at, :].astype(F32)
            b = b + lk[chips + n - 1, one, :] * ends[n, bt, :].astype(F32)
        state[at, :] = s
        back[at, :] = b
        fs[0, at, :] = s.astype(BF16)
        bs[0, at, :] = b.astype(BF16)
        return 0

    def ring(src, dst, sem, device):
        moves = []
        for n in range(REACH):
            pair = []
            for part in range(2):
                at = pl.ds(part * columns // 2, columns // 2)
                k = sem + 2 * n + part
                pair.append(remote(src.at[n, at, :], dst.at[n, at, :], ring_ssem.at[k], ring_rsem.at[k], device))
            moves.append(pair)
        return moves

    fwd = ring(fs, fr, REACH, after)
    bwd = ring(bs, br, 3 * REACH, ahead)

    def over(part, body):
        lax.fori_loop(part * heads // 2, (part + 1) * heads // 2, body, 0)

    for part in range(2):
        over(part, totals)
        fwd[0][part].start()
        bwd[0][part].start()
    hops[1].wait_recv()
    hops[2].start()
    for n in range(1, REACH):
        for part in range(2):
            for moves, base, recv, send in ((bwd, back, br, bs), (fwd, state, fr, fs)):
                moves[n - 1][part].wait_recv()

                def step(h, _):
                    at, unused = head_rows(h)
                    val = base[at, :] + lk[whole, pl.ds(h, 1), :] * recv[n - 1, at, :].astype(F32)
                    send[n, at, :] = val.astype(BF16)
                    return 0

                over(part, step)
                moves[n][part].start()

    def chip_states(h, _):
        at, bt = head_rows(h)
        one = pl.ds(h, 1)
        s = fr[REACH - 1, at, :].astype(F32)
        b = br[REACH - 1, at, :].astype(F32)
        for n in range(chips):
            both[n, at, :] = s.astype(BF16)
            s = lk[n, one, :] * s + ends[n, at, :].astype(F32)
        for n in reversed(range(chips)):
            both[n, bt, :] = b.astype(BF16)
            b = lk[n, one, :] * b + ends[n, bt, :].astype(F32)
        return 0

    for part in range(2):
        bwd[REACH - 1][part].wait_recv()
        fwd[REACH - 1][part].wait_recv()
        over(part, chip_states)
    hops[REACH - 1].wait_recv()
    for c in qg_own + outs + more:
        c.wait()
    for c in qg_moves:
        c.wait_recv()
    for c in pairs + kv_moves + qg_moves + end_moves + hops + sum(fwd + bwd, []):
        c.wait_send()


def first_stage(lengths, slow, x, g, w, r, st, q, k, v, ag, fast, gains, parts, cores):
    chips = parts // cores
    tokens = x.shape[0]
    rows = tokens * parts
    half, thin = x.shape[1] // cores, w.shape[1] // cores
    columns = half // chips
    heads = columns // HD
    packed = 2 * columns + 2 * heads
    both_rows = cores * tokens
    hbm = pl.BlockSpec(memory_space=pltpu.HBM)
    vmem = pl.BlockSpec(memory_space=pltpu.VMEM)
    dma = pltpu.SemaphoreType.DMA
    return pl.pallas_call(
        first_kernel,
        in_specs=[pl.BlockSpec(memory_space=pltpu.SMEM)] * 2 + [hbm] * 9 + [vmem] * 2,
        out_specs=[hbm] * 9 + [vmem],
        out_shape=[
            jax.ShapeDtypeStruct((both_rows, half), BF16),
            jax.ShapeDtypeStruct((both_rows, half), BF16),
            jax.ShapeDtypeStruct((both_rows, thin), BF16),
            jax.ShapeDtypeStruct((both_rows, st.shape[1]), BF16),
            jax.ShapeDtypeStruct((both_rows, half), F32),
            jax.ShapeDtypeStruct((both_rows, thin), F32),
            jax.ShapeDtypeStruct((both_rows, thin), F32),
            jax.ShapeDtypeStruct(((REACH + 1) * rows, 2 * DH), BF16),
            jax.ShapeDtypeStruct((rows, 2 * q.shape[1] // parts), BF16),
            jax.ShapeDtypeStruct((chips, 2 * columns, NS), BF16),
        ],
        scratch_shapes=[
            pltpu.VMEM((both_rows, half), BF16),
            pltpu.VMEM((both_rows, half), BF16),
            pltpu.VMEM((both_rows, thin), BF16),
            pltpu.VMEM((both_rows, thin), BF16),
            pltpu.VMEM((both_rows, st.shape[1]), BF16),
            pltpu.VMEM((both_rows, half), F32),
            pltpu.VMEM((both_rows, thin), F32),
            pltpu.VMEM((both_rows, thin), F32),
            pltpu.VMEM((128, both_rows), F32),
            pltpu.VMEM((chips - 1, packed, NS), BF16),
            pltpu.VMEM((chips, packed, NS), BF16),
            pltpu.VMEM((2 * chips, heads, 128), F32),
            pltpu.VMEM((columns, NS), F32),
            pltpu.VMEM((columns, NS), F32),
            pltpu.VMEM((REACH, columns, NS), BF16),
            pltpu.VMEM((REACH, columns, NS), BF16),
            pltpu.VMEM((REACH, columns, NS), BF16),
            pltpu.VMEM((REACH, columns, NS), BF16),
            dma((9,)),
            dma((5,)),
            dma((5,)),
            dma((4, parts)),
            dma((4, parts)),
            dma((chips,)),
            dma((chips,)),
            dma((REACH * 5,)),
            dma((REACH * 5,)),
            dma((7,)),
        ],
        compiler_params=pltpu.CompilerParams(vmem_limit_bytes=60 << 20, collective_id=0, has_side_effects=True),
        cost_estimate=pl.CostEstimate(flops=2 * 10**9, bytes_accessed=16 << 20, transcendentals=10**5),
        name="first_stage",
    )(lengths, slow, x, g, w, r, st, q, k, v, ag, fast, gains)


def last_kernel(
    lengths, slow, x, g, w, st, fast, inner_x, inner_w, inner_r, both, grad_q, out_x, out_w, out_r, out_q,
    entering, to_end, res_x, res_w, res_r, own_sem, pair_send, pair_recv, q_send, q_recv,
):
    j = pl.program_id(0)
    ctx, hx, core = lax.axis_index("ctx"), lax.axis_index("hx"), lax.axis_index("core")
    chips, cores = lax.axis_size("hx"), lax.axis_size("core")
    parts = chips * cores
    me = hx * cores + core
    other = 1 - core
    tokens = out_x.shape[0]
    columns = x.shape[1]
    heads = columns // HD
    qw = grad_q.shape[1]
    begin = ctx * tokens * parts + hx * BLOCK
    group = core * chips + j
    starts = starts_of(lengths)

    def cols(n, width):
        return pl.ds(pl.multiple_of(n * width, 128), width)

    def remote(src, dst, ssem, rsem, device):
        return pltpu.make_async_remote_copy(
            src_ref=src, dst_ref=dst, send_sem=ssem, recv_sem=rsem, device_id=device, device_id_type=MESH
        )

    def q_moves():
        moves = []
        for d in range(1, parts):
            p = lax.rem(me + d, parts)
            device = {"hx": p // cores, "core": lax.rem(p, cores)}
            moves.append(remote(grad_q.at[cols(p, tokens), :], out_q.at[:, cols(me, qw)], q_send.at[d], q_recv.at[d], device))
        own = pltpu.make_async_copy(grad_q.at[cols(me, tokens), :], out_q.at[:, cols(me, qw)], own_sem.at[chips, 0])
        return moves, own

    def pair_moves(n):
        moves, owns = [], []
        for k, (res, out, width) in enumerate(((res_x, out_x, columns), (res_w, out_w, NS), (res_r, out_r, NS))):
            place = out.at[:, cols(core * chips + n, width)]
            moves.append(
                remote(res.at[n, cols(other, tokens), :], place, pair_send.at[n, k], pair_recv.at[n, k], {"core": other})
            )
            owns.append(pltpu.make_async_copy(res.at[n, cols(core, tokens), :], place, own_sem.at[n, k]))
        return moves, owns

    @pl.when(j == 0)
    def _():
        barrier = pltpu.get_barrier_semaphore()
        for d in range(1, parts):
            p = lax.rem(me + d, parts)
            pl.semaphore_signal(
                barrier, inc=1, device_id={"hx": p // cores, "core": lax.rem(p, cores)}, device_id_type=MESH
            )
        pl.semaphore_wait(barrier, parts - 1)
        moves, own = q_moves()
        for c in moves + [own]:
            c.start()
        _, b, c, _ = edges(starts, begin, 0, st[...], rates_of(slow, fast, tokens * parts * lax.axis_size("ctx")))
        entering[...] = b
        to_end[...] = c

    spread = spread_matrix(columns, group)
    end_wide = widen(to_end[...], spread)
    iw = (x[...].astype(F32) * end_wide).astype(BF16)
    gw = (g[...].astype(F32) * widen(entering[...], spread)).astype(BF16)
    state = both[0, 0:columns, :]
    back = both[0, columns : 2 * columns, :]
    res_x[j] = (inner_x[...] + end_wide * dot_nt(w[...], back)).astype(BF16)
    res_w[j] = (inner_w[...] + dot_nn(iw, back)).astype(BF16)
    res_r[j] = (inner_r[...] + dot_nn(gw, state)).astype(BF16)

    for n in range(chips):

        @pl.when(j == n)
        def _():
            moves, owns = pair_moves(n)
            for c in moves + owns:
                c.start()

    @pl.when(j == chips - 1)
    def _():
        moves, own = q_moves()
        own.wait()
        for c in moves:
            c.wait_recv()
        for c in moves:
            c.wait_send()
        for n in range(chips):
            moves, owns = pair_moves(n)
            for c in owns:
                c.wait()
            for c in moves:
                c.wait_recv()
            for c in moves:
                c.wait_send()


def last_stage(lengths, slow, mix, fast, inner, both, grad_q, parts, cores):
    chips = both.shape[0]
    columns = both.shape[1] // 2
    tokens = BLOCK // cores
    groups = chips * cores
    hbm = pl.BlockSpec(memory_space=pltpu.HBM)
    dma = pltpu.SemaphoreType.DMA
    return pl.pallas_call(
        last_kernel,
        grid_spec=pltpu.PrefetchScalarGridSpec(
            num_scalar_prefetch=2,
            grid=(chips,),
            in_specs=[
                pl.BlockSpec((BLOCK, columns), lambda j, *_: (0, j)),
                pl.BlockSpec((BLOCK, columns), lambda j, *_: (0, j)),
                pl.BlockSpec((BLOCK, NS), lambda j, *_: (0, j)),
                pl.BlockSpec((BLOCK, 128), lambda j, *_: (0, 0)),
                pl.BlockSpec((1, 128), lambda j, *_: (0, 0)),
                pl.BlockSpec((BLOCK, columns), lambda j, *_: (0, j)),
                pl.BlockSpec((BLOCK, NS), lambda j, *_: (0, j)),
                pl.BlockSpec((BLOCK, NS), lambda j, *_: (0, j)),
                pl.BlockSpec((1, 2 * columns, NS), lambda j, *_: (j, 0, 0)),
                hbm,
            ],
            out_specs=[hbm] * 4,
            scratch_shapes=[
                pltpu.VMEM((BLOCK, 128), F32),
                pltpu.VMEM((BLOCK, 128), F32),
                pltpu.VMEM((chips, BLOCK, columns), BF16),
                pltpu.VMEM((chips, BLOCK, NS), BF16),
                pltpu.VMEM((chips, BLOCK, NS), BF16),
                dma((chips + 1, 3)),
                dma((chips, 3)),
                dma((chips, 3)),
                dma((parts,)),
                dma((parts,)),
            ],
        ),
        out_shape=[
            jax.ShapeDtypeStruct((tokens, groups * columns), BF16),
            jax.ShapeDtypeStruct((tokens, groups * NS), BF16),
            jax.ShapeDtypeStruct((tokens, groups * NS), BF16),
            jax.ShapeDtypeStruct((tokens, parts * grad_q.shape[1]), BF16),
        ],
        compiler_params=pltpu.CompilerParams(vmem_limit_bytes=56 << 20, collective_id=1, has_side_effects=True),
        cost_estimate=pl.CostEstimate(flops=8 * 10**9, bytes_accessed=14 << 20, transcendentals=5 * 10**6),
        name="last_stage",
    )(lengths, slow, *mix, fast, *inner, both, grad_q)


HEAD = ("hx", "core")


def shards(x, w, r, steps, fast_rates, slow_heads, skip_gains, grad, q, k, v, ag, doc_lengths):
    parts = lax.axis_size(HEAD)
    cores = lax.axis_size("core")
    slab_first = (lax.axis_index("ctx") * x.shape[0] * parts).astype(jnp.int32).reshape(1)
    fast = fast_rates.reshape(1, MH)
    gains = skip_gains.reshape(1, MH)
    *mix, kv, qg, both = first_stage(
        doc_lengths, slow_heads, x, grad, w, r, steps, q, k, v, ag, fast, gains, parts, cores
    )
    mix, inner = mix[:4], mix[4:]
    both = lax.all_to_all(both, "hx", split_axis=0, concat_axis=0, tiled=True)
    grad_q = attention(qg, kv, doc_lengths, slab_first)
    return tuple(last_stage(doc_lengths, slow_heads, mix, fast, inner, both, grad_q, parts, cores))


def solution(mesh):
    split = Mesh(mesh.devices.reshape(mesh.shape["ctx"], -1, 2), ("ctx", "hx", "core"))
    tokens = P(("ctx", "hx", "core"), None)
    return jax.shard_map(
        shards,
        mesh=split,
        in_specs=(tokens, tokens, tokens, tokens, P(), P(), P(), tokens, tokens, tokens, tokens, tokens, P()),
        out_specs=(tokens, tokens, tokens, tokens),
        check_vma=False,
    )
```

```python
import functools

import jax
import jax.numpy as jnp
from jax import lax
from jax.experimental import pallas as pl
from jax.experimental.pallas import tpu as pltpu
from jax.sharding import Mesh
from jax.sharding import PartitionSpec as P

MH = 128
HD = 64
NS = 128
DH = 128
BLOCK = 256
LOG2E = 1.4426950408889634
REACH = 3
QB = 256
KB = 512
SUB = 256
EARLY = 0
NEG = -1e30

F32 = jnp.float32
BF16 = jnp.bfloat16


def dot_nt(a, b):
    return lax.dot_general(a, b, (((1,), (1,)), ((), ())), preferred_element_type=F32)


def dot_nn(a, b):
    return lax.dot_general(a, b, (((1,), (0,)), ((), ())), preferred_element_type=F32)


def dot_tn(a, b):
    return lax.dot_general(a, b, (((0,), (0,)), ((), ())), preferred_element_type=F32)


def attention_kernel(lengths, first, qg, kv_all, out, kv, kt, turned, e_scr, gp_scr, tops, sems):
    i = pl.program_id(0)
    rows = kv_all.shape[0] // (REACH + 1)
    lead = REACH * rows
    heads = out.shape[1] // DH

    @pl.when(i == 0)
    def _():
        c = pltpu.make_async_copy(kv_all, kv.at[pl.ds(KB, kv_all.shape[0]), :], sems.at[0])
        c.start()
        kv[0:KB, :] = jnp.zeros((KB, 2 * DH), BF16)
        c.wait()

        def turn(n, _):
            at = pl.ds(pl.multiple_of(n * KB, KB), KB)
            kt[:, at] = jnp.transpose(kv[at, 0:DH])
            return 0

        lax.fori_loop(0, kv.shape[0] // KB, turn, 0)

    for h in range(2 * heads):
        turned[h] = jnp.transpose(qg[:, h * DH : (h + 1) * DH])

    base = first[0] - lead
    q0 = lead + i * QB
    qrow = q0 + iota((1, QB), 1)
    drow = jnp.zeros((1, QB), jnp.int32)
    low = jnp.int32(0)
    high = jnp.int32(0)
    for start in starts_of(lengths):
        st = start - base
        low = jnp.where(st <= q0, st, low)
        high = jnp.where(st <= q0 + QB - 1, st, high)
        drow = jnp.where(st <= qrow, st, drow)
    end = q0 + QB
    blocks = (end - low + KB - 1) // KB
    begin = end - blocks * KB
    edge = blocks - 1
    full = jnp.minimum((high - begin + KB - 1) // KB, edge)
    scale = DH**-0.5 * LOG2E

    def fold(x):
        return x.reshape(-1, 8, QB)

    def place(b, n):
        return pl.ds(pl.multiple_of(KB + begin + b * KB + n * SUB, 128), SUB)

    def forward(masked, b, carry):
        new = []
        for h in range(heads):
            top, total, mean = carry[h]
            for n in range(KB // SUB):
                at = place(b, n)
                s = dot_nn(kv[at, 0:DH], turned[h])
                if masked:
                    key = begin + b * KB + n * SUB + iota((SUB, QB), 0)
                    s = jnp.where((key >= drow) & (key <= qrow), s, NEG)
                last = top
                top = jnp.maximum(top, jnp.max(jnp.max(fold(s), axis=0), axis=0, keepdims=True))
                e = jnp.exp2((s - top) * scale)
                gp = dot_nn(kv[at, DH : 2 * DH], turned[heads + h])
                part = slice(n * SUB, (n + 1) * SUB)
                e_scr[b, h, part, :] = e
                gp_scr[b, h, part, :] = gp
                tops[b, h, n] = jnp.broadcast_to(top, (8, QB))
                fade = jnp.exp2((last - top) * scale)
                total = total * fade + jnp.sum(fold(e), axis=0)
                mean = mean * fade + jnp.sum(fold(e * gp), axis=0)
            new.append((top, total, mean))
        return tuple(new)

    zero = jnp.zeros((8, QB), F32)
    carry = ((jnp.full((1, QB), NEG, F32), zero, zero),) * heads
    carry = lax.fori_loop(0, full, functools.partial(forward, True), carry)
    carry = lax.fori_loop(full, edge, functools.partial(forward, False), carry)
    carry = forward(True, edge, carry)
    peak = [c[0] for c in carry]
    total = [jnp.sum(c[1], axis=0, keepdims=True) for c in carry]
    centre = [jnp.sum(c[2], axis=0, keepdims=True) / t for c, t in zip(carry, total)]

    def grads(b, accs):
        new = []
        for h in range(heads):
            acc = accs[h]
            for n in range(KB // SUB):
                part = slice(n * SUB, (n + 1) * SUB)
                ds = (e_scr[b, h, part, :] * (gp_scr[b, h, part, :] - centre[h])).astype(BF16)
                fade = jnp.exp2((tops[b, h, n, 0:1, :] - peak[h]) * scale)
                acc += dot_nn(kt[:, place(b, n)], ds) * fade
            new.append(acc)
        return tuple(new)

    accs = lax.fori_loop(0, blocks, grads, (jnp.zeros((DH, QB), F32),) * heads)
    for h in range(heads):
        res = accs[h] * (DH**-0.5 / total[h])
        out[:, h * DH : (h + 1) * DH] = jnp.transpose(res).astype(BF16)


def attention(qg, kv, lengths, first):
    rows = qg.shape[0]
    heads = qg.shape[1] // (2 * DH)
    lead = REACH * rows
    most = (lead + QB - 1 + KB - 1) // KB
    return pl.pallas_call(
        attention_kernel,
        grid_spec=pltpu.PrefetchScalarGridSpec(
            num_scalar_prefetch=2,
            grid=(rows // QB,),
            in_specs=[
                pl.BlockSpec((QB, qg.shape[1]), lambda i, *_: (i, 0)),
                pl.BlockSpec(memory_space=pltpu.HBM),
            ],
            out_specs=pl.BlockSpec((QB, heads * DH), lambda i, *_: (i, 0)),
            scratch_shapes=[
                pltpu.VMEM((KB + lead + rows, 2 * DH), BF16),
                pltpu.VMEM((DH, KB + lead + rows), BF16),
                pltpu.VMEM((2 * heads, DH, QB), BF16),
                pltpu.VMEM((most, heads, KB, QB), F32),
                pltpu.VMEM((most, heads, KB, QB), F32),
                pltpu.VMEM((most, heads, KB // SUB, 8, QB), F32),
                pltpu.SemaphoreType.DMA((1,)),
            ],
        ),
        out_shape=jax.ShapeDtypeStruct((rows, heads * DH), BF16),
        compiler_params=pltpu.CompilerParams(vmem_limit_bytes=58 << 20),
        cost_estimate=pl.CostEstimate(flops=12 * 10**9, bytes_accessed=6 << 20, transcendentals=16 * 10**6),
        name="attention",
    )(lengths, first, qg, kv)


def split_sum(tri, dl):
    a = dl.astype(BF16)
    rest = dl - a.astype(F32)
    b = rest.astype(BF16)
    c = (rest - b.astype(F32)).astype(BF16)
    return dot_nn(tri, a) + dot_nn(tri, b) + dot_nn(tri, c)


def iota(shape, dim):
    return lax.broadcasted_iota(jnp.int32, shape, dim)


def starts_of(lengths):
    starts = [jnp.int32(0)]
    for j in range(lengths.shape[0] - 1):
        starts.append(starts[-1] + lengths[j])
    return starts


def rates_of(slow, fast, total_rows):
    rates = fast[...]
    lane = iota(rates.shape, 1)
    for n in range(slow.shape[0]):
        rates = jnp.where(lane == slow[n], 1.0 / total_rows, rates)
    return rates * -LOG2E


def doc_of(starts, pos):
    d = jnp.zeros(pos.shape, jnp.int32)
    for st in starts:
        d += (st <= pos).astype(jnp.int32)
    return d


def widen(values, spread):
    hi = values.astype(BF16)
    lo = (values - hi.astype(F32)).astype(BF16)
    return dot_nn(hi, spread) + dot_nn(lo, spread)


def edges(starts, first, c, st, rates):
    tri = (iota((BLOCK, BLOCK), 0) >= iota((BLOCK, BLOCK), 1)).astype(BF16)
    cum = split_sum(tri, st.astype(F32) * rates)
    begin = first + c * BLOCK
    doc_col = doc_of(starts, begin + iota((BLOCK, 1), 0))
    doc_last = doc_of(starts, begin + BLOCK - 1 + iota((1, 1), 0))
    doc_prev = doc_of(starts, begin - 1 + iota((1, 1), 0))
    total = cum[BLOCK - 1 : BLOCK, :]
    entering = jnp.exp2(jnp.where(doc_col == doc_prev, cum, NEG))
    to_end = jnp.exp2(jnp.where(doc_col == doc_last, total - cum, NEG))
    return cum, entering, to_end, doc_last == doc_prev


def spread_matrix(columns, group):
    return (iota((128, columns), 0) == group * (columns // HD) + iota((128, columns), 1) // HD).astype(BF16)


MESH = pl.DeviceIdType.MESH


def links_of(rows):
    n = rows.shape[0] // 2
    return rows[0:n, :].astype(F32) + rows[n : 2 * n, :].astype(F32)


def first_kernel(
    lengths, slow, x, g, w, r, st, q, k, v, ag, fast, gains,
    xs_out, gs_out, ws_out, st_out, ix_out, iw_out, ir_out, kv_out, qg_out, both,
    kv, qg, xs, gs, ws, rs, sts, ix, iw_in, ir_in, cum_t, ends_send, ends, lk, state, back, fs, fr, bs, br,
    own_sem, pair_send, pair_recv, head_send, head_recv, ends_ssem, ends_rsem, ring_ssem, ring_rsem, out_sem,
):
    ctx, hx, core = lax.axis_index("ctx"), lax.axis_index("hx"), lax.axis_index("core")
    slabs, chips, cores = lax.axis_size("ctx"), lax.axis_size("hx"), lax.axis_size("core")
    parts = chips * cores
    me = hx * cores + core
    other = 1 - core
    tokens = x.shape[0]
    rows = tokens * parts
    half = x.shape[1] // cores
    thin = w.shape[1] // cores
    qw = q.shape[1] // parts
    columns = half // chips
    heads = columns // HD
    begin = ctx * rows + hx * BLOCK
    starts = starts_of(lengths)

    def peer(d):
        p = lax.rem(me + d, parts)
        return p, {"hx": p // cores, "core": lax.rem(p, cores)}

    after = {"ctx": lax.rem(ctx + 1, slabs)}
    ahead = {"ctx": lax.rem(ctx + slabs - 1, slabs)}

    barrier = pltpu.get_barrier_semaphore()
    for d in range(1, parts):
        pl.semaphore_signal(barrier, inc=1, device_id=peer(d)[1], device_id_type=MESH)
    for n in (after, ahead):
        pl.semaphore_signal(barrier, inc=1, device_id=n, device_id_type=MESH)
    pl.semaphore_wait(barrier, parts + 1)

    def remote(src, dst, ssem, rsem, device):
        return pltpu.make_async_remote_copy(
            src_ref=src, dst_ref=dst, send_sem=ssem, recv_sem=rsem, device_id=device, device_id_type=MESH
        )

    def cols(n, width):
        return pl.ds(pl.multiple_of(n * width, 128), width)

    mine = pl.ds(pl.multiple_of(core * tokens, 128), tokens)
    pairs, owns = [], []
    for n, (src, dst, width) in enumerate(((x, xs, half), (g, gs, half), (w, ws, thin), (r, rs, thin), (st, sts, None))):
        theirs = src if width is None else src.at[:, cols(other, width)]
        ours = src if width is None else src.at[:, cols(core, width)]
        pairs.append(remote(theirs, dst.at[mine, :], pair_send.at[n], pair_recv.at[n], {"core": other}))
        owns.append(pltpu.make_async_copy(ours, dst.at[mine, :], own_sem.at[n]))
    for c in pairs + owns:
        c.start()
    lead = REACH * rows
    mine_kv = pl.ds(pl.multiple_of(lead + me * tokens, 128), tokens)
    mine_q = pl.ds(pl.multiple_of(me * tokens, 128), tokens)
    kv_moves, qg_moves, kv_own, qg_own = [], [], [], []
    for n, (src, dst, width, at, into, own) in enumerate(
        (
            (k, kv, DH, mine_kv, kv_moves, kv_own),
            (v, kv, DH, mine_kv, kv_moves, kv_own),
            (q, qg, qw, mine_q, qg_moves, qg_own),
            (ag, qg, qw, mine_q, qg_moves, qg_own),
        )
    ):
        place = slice((n % 2) * width, (n % 2 + 1) * width)
        for d in range(1, parts):
            p, device = peer(d)
            into.append(
                remote(src.at[:, cols(p, width)], dst.at[at, place], head_send.at[n, d], head_recv.at[n, d], device)
            )
        own.append(pltpu.make_async_copy(src.at[:, cols(me, width)], dst.at[at, place], own_sem.at[5 + n]))
    for c in kv_moves + kv_own + qg_own + qg_moves[:EARLY]:
        c.start()

    for c in owns:
        c.wait()
    for c in pairs:
        c.wait_recv()
    outs = [
        pltpu.make_async_copy(src, dst, out_sem.at[n])
        for n, (src, dst) in enumerate(((xs, xs_out), (gs, gs_out), (ws, ws_out), (sts, st_out)))
    ]
    for c in outs:
        c.start()

    cum, entering, to_end, linked = edges(starts, begin, 0, sts[...], rates_of(slow, fast, rows * slabs))
    entering_hi = entering.astype(BF16)
    entering_lo = (entering - entering_hi.astype(F32)).astype(BF16)
    to_end_hi = to_end.astype(BF16)
    to_end_lo = (to_end - to_end_hi.astype(F32)).astype(BF16)
    tot = jnp.transpose(jnp.broadcast_to(cum[BLOCK - 1 : BLOCK, :], (128, 128)))
    link_all = jnp.exp2(jnp.where(linked, tot, NEG))

    def make_ends(group, out):
        spread = spread_matrix(columns, core * chips + group)
        wide_end = dot_nn(to_end_hi, spread) + dot_nn(to_end_lo, spread)
        wide_enter = dot_nn(entering_hi, spread) + dot_nn(entering_lo, spread)
        iw = (xs[:, cols(group, columns)].astype(F32) * wide_end).astype(BF16)
        gw = (gs[:, cols(group, columns)].astype(F32) * wide_enter).astype(BF16)
        out[0:columns, :] = dot_tn(iw, ws[:, cols(group, NS)]).astype(BF16)
        out[columns : 2 * columns, :] = dot_tn(gw, rs[:, cols(group, NS)]).astype(BF16)
        pick = (iota((heads, 128), 1) == (core * chips + group) * heads + iota((heads, 128), 0)).astype(F32)
        link = lax.dot_general(
            pick, link_all, (((1,), (0,)), ((), ())), precision=lax.Precision.HIGHEST, preferred_element_type=F32
        )
        hi = link.astype(BF16)
        out[2 * columns : 2 * columns + heads, :] = hi
        out[2 * columns + heads : 2 * columns + 2 * heads, :] = (link - hi.astype(F32)).astype(BF16)

    hops = []
    for n in range(REACH):
        src = pl.ds((REACH - n) * rows, rows)
        dst = pl.ds((REACH - n - 1) * rows, rows)
        hops.append(remote(kv.at[src, :], kv.at[dst, :], ring_ssem.at[n], ring_rsem.at[n], after))

    end_moves = []
    for d in range(1, chips):
        to = lax.rem(hx + d, chips)
        make_ends(to, ends_send.at[d - 1])
        c = remote(ends_send.at[d - 1], ends.at[hx], ends_ssem.at[d], ends_rsem.at[d], {"hx": to})
        c.start()
        end_moves.append(c)
        if d == 1:
            for c in kv_own:
                c.wait()
            for c in kv_moves:
                c.wait_recv()
            hops[0].start()
    make_ends(hx, ends.at[hx])

    cum_t[...] = jnp.transpose(cum)
    doc_col = doc_of(starts, begin + iota((BLOCK, 1), 0))
    doc_row = doc_of(starts, begin + iota((1, BLOCK), 1))
    ok = (iota((BLOCK, BLOCK), 0) <= iota((BLOCK, BLOCK), 1)) & (doc_col == doc_row)
    lane = iota((BLOCK, 2 * HD), 1) < HD

    def inside(group, _):
        spread = spread_matrix(columns, core * chips + group)
        skips = widen(jnp.broadcast_to(gains[...], (8, 128)), spread)[0:1, :]
        wv = ws[:, cols(group, NS)]
        rv = rs[:, cols(group, NS)]
        scores = dot_nt(wv, rv)
        joint = jnp.zeros((BLOCK, BLOCK), F32)
        offset = pl.multiple_of((core * chips + group) * heads, heads)
        rows_t = cum_t[pl.ds(offset, heads), :]
        cols_t = jnp.transpose(jnp.concatenate([rows_t, jnp.zeros((128 - heads, BLOCK), F32)], axis=0))
        for p in range(heads // 2):
            at = pl.ds(pl.multiple_of(group * columns + p * 2 * HD, 2 * HD), 2 * HD)
            xp = xs[:, at]
            gp = gs[:, at]
            zero = jnp.zeros_like(xp)
            inner = skips[:, p * 2 * HD : (p + 1) * 2 * HD] * gp.astype(F32)
            for part in range(2):
                h = 2 * p + part
                mine = lane if part == 0 else ~lane
                decay = jnp.exp2(jnp.where(ok, rows_t[h : h + 1, :] - cols_t[:, h : h + 1], NEG))
                joint += decay * dot_nt(jnp.where(mine, xp, zero), gp)
                mixing = (scores * decay).astype(BF16)
                inner += dot_nn(mixing, jnp.where(mine, gp, zero))
            ix[:, at] = inner
        low = joint.astype(BF16)
        iw_in[:, cols(group, NS)] = dot_nn(low, rv)
        ir_in[:, cols(group, NS)] = dot_tn(low, wv)
        return 0

    lax.fori_loop(0, chips // 2, inside, 0)
    hops[0].wait_recv()
    hops[1].start()
    lax.fori_loop(chips // 2, chips, inside, 0)
    more = [
        pltpu.make_async_copy(src, dst, out_sem.at[4 + n])
        for n, (src, dst) in enumerate(((ix, ix_out), (iw_in, iw_out), (ir_in, ir_out)))
    ]
    for c in more:
        c.start()

    for c in end_moves:
        c.wait_recv()
    for c in qg_moves[EARLY:]:
        c.start()
    for n in range(chips):
        lk[n] = links_of(ends[n, 2 * columns :, :])
    prods = [None, lk[0]]
    for n in range(1, chips):
        prods.append(prods[-1] * lk[n])
    for n in range(1, chips + 1):
        lk[chips + n - 1] = prods[n]
    whole = 2 * chips - 1

    def head_rows(h):
        return pl.ds(pl.multiple_of(h * HD, HD), HD), pl.ds(pl.multiple_of(columns + h * HD, HD), HD)

    def totals(h, _):
        at, bt = head_rows(h)
        one = pl.ds(h, 1)
        s = ends[0, at, :].astype(F32)
        b = ends[0, bt, :].astype(F32)
        for n in range(1, chips):
            s = lk[n, one, :] * s + ends[n, at, :].astype(F32)
            b = b + lk[chips + n - 1, one, :] * ends[n, bt, :].astype(F32)
        state[at, :] = s
        back[at, :] = b
        fs[0, at, :] = s.astype(BF16)
        bs[0, at, :] = b.astype(BF16)
        return 0

    def ring(src, dst, sem, device):
        moves = []
        for n in range(REACH):
            pair = []
            for part in range(2):
                at = pl.ds(part * columns // 2, columns // 2)
                k = sem + 2 * n + part
                pair.append(remote(src.at[n, at, :], dst.at[n, at, :], ring_ssem.at[k], ring_rsem.at[k], device))
            moves.append(pair)
        return moves

    fwd = ring(fs, fr, REACH, after)
    bwd = ring(bs, br, 3 * REACH, ahead)

    def over(part, body):
        lax.fori_loop(part * heads // 2, (part + 1) * heads // 2, body, 0)

    for part in range(2):
        over(part, totals)
        fwd[0][part].start()
        bwd[0][part].start()
    for n in range(1, REACH):
        for part in range(2):
            for moves, base, recv, send in ((bwd, back, br, bs), (fwd, state, fr, fs)):
                moves[n - 1][part].wait_recv()

                def step(h, _):
                    at, unused = head_rows(h)
                    val = base[at, :] + lk[whole, pl.ds(h, 1), :] * recv[n - 1, at, :].astype(F32)
                    send[n, at, :] = val.astype(BF16)
                    return 0

                over(part, step)
                moves[n][part].start()
    hops[1].wait_recv()
    hops[2].start()

    def chip_states(h, _):
        at, bt = head_rows(h)
        one = pl.ds(h, 1)
        s = fr[REACH - 1, at, :].astype(F32)
        b = br[REACH - 1, at, :].astype(F32)
        for n in range(chips):
            both[n, at, :] = s.astype(BF16)
            s = lk[n, one, :] * s + ends[n, at, :].astype(F32)
        for n in reversed(range(chips)):
            both[n, bt, :] = b.astype(BF16)
            b = lk[n, one, :] * b + ends[n, bt, :].astype(F32)
        return 0

    for part in range(2):
        bwd[REACH - 1][part].wait_recv()
        fwd[REACH - 1][part].wait_recv()
        over(part, chip_states)
    hops[REACH - 1].wait_recv()
    kv_back = pltpu.make_async_copy(kv, kv_out, out_sem.at[7])
    kv_back.start()
    for c in qg_own + outs + more:
        c.wait()
    for c in qg_moves:
        c.wait_recv()
    qg_back = pltpu.make_async_copy(qg, qg_out, out_sem.at[8])
    qg_back.start()
    kv_back.wait()
    qg_back.wait()
    for c in pairs + kv_moves + qg_moves + end_moves + hops + sum(fwd + bwd, []):
        c.wait_send()


def first_stage(lengths, slow, x, g, w, r, st, q, k, v, ag, fast, gains, parts, cores):
    chips = parts // cores
    tokens = x.shape[0]
    rows = tokens * parts
    half, thin = x.shape[1] // cores, w.shape[1] // cores
    columns = half // chips
    heads = columns // HD
    packed = 2 * columns + 2 * heads
    both_rows = cores * tokens
    hbm = pl.BlockSpec(memory_space=pltpu.HBM)
    vmem = pl.BlockSpec(memory_space=pltpu.VMEM)
    dma = pltpu.SemaphoreType.DMA
    return pl.pallas_call(
        first_kernel,
        in_specs=[pl.BlockSpec(memory_space=pltpu.SMEM)] * 2 + [hbm] * 5 + [vmem] * 6,
        out_specs=[hbm] * 9 + [vmem],
        out_shape=[
            jax.ShapeDtypeStruct((both_rows, half), BF16),
            jax.ShapeDtypeStruct((both_rows, half), BF16),
            jax.ShapeDtypeStruct((both_rows, thin), BF16),
            jax.ShapeDtypeStruct((both_rows, st.shape[1]), BF16),
            jax.ShapeDtypeStruct((both_rows, half), F32),
            jax.ShapeDtypeStruct((both_rows, thin), F32),
            jax.ShapeDtypeStruct((both_rows, thin), F32),
            jax.ShapeDtypeStruct(((REACH + 1) * rows, 2 * DH), BF16),
            jax.ShapeDtypeStruct((rows, 2 * q.shape[1] // parts), BF16),
            jax.ShapeDtypeStruct((chips, 2 * columns, NS), BF16),
        ],
        scratch_shapes=[
            pltpu.VMEM(((REACH + 1) * rows, 2 * DH), BF16),
            pltpu.VMEM((rows, 2 * q.shape[1] // parts), BF16),
            pltpu.VMEM((both_rows, half), BF16),
            pltpu.VMEM((both_rows, half), BF16),
            pltpu.VMEM((both_rows, thin), BF16),
            pltpu.VMEM((both_rows, thin), BF16),
            pltpu.VMEM((both_rows, st.shape[1]), BF16),
            pltpu.VMEM((both_rows, half), F32),
            pltpu.VMEM((both_rows, thin), F32),
            pltpu.VMEM((both_rows, thin), F32),
            pltpu.VMEM((128, both_rows), F32),
            pltpu.VMEM((chips - 1, packed, NS), BF16),
            pltpu.VMEM((chips, packed, NS), BF16),
            pltpu.VMEM((2 * chips, heads, 128), F32),
            pltpu.VMEM((columns, NS), F32),
            pltpu.VMEM((columns, NS), F32),
            pltpu.VMEM((REACH, columns, NS), BF16),
            pltpu.VMEM((REACH, columns, NS), BF16),
            pltpu.VMEM((REACH, columns, NS), BF16),
            pltpu.VMEM((REACH, columns, NS), BF16),
            dma((9,)),
            dma((5,)),
            dma((5,)),
            dma((4, parts)),
            dma((4, parts)),
            dma((chips,)),
            dma((chips,)),
            dma((REACH * 5,)),
            dma((REACH * 5,)),
            dma((9,)),
        ],
        compiler_params=pltpu.CompilerParams(vmem_limit_bytes=60 << 20, collective_id=0, has_side_effects=True),
        cost_estimate=pl.CostEstimate(flops=2 * 10**9, bytes_accessed=16 << 20, transcendentals=10**5),
        name="first_stage",
    )(lengths, slow, x, g, w, r, st, q, k, v, ag, fast, gains)


def last_kernel(
    lengths, slow, x, g, w, st, fast, inner_x, inner_w, inner_r, both, grad_q, out_x, out_w, out_r, out_q,
    entering, to_end, res_x, res_w, res_r, own_sem, pair_send, pair_recv, q_send, q_recv,
):
    j = pl.program_id(0)
    ctx, hx, core = lax.axis_index("ctx"), lax.axis_index("hx"), lax.axis_index("core")
    chips, cores = lax.axis_size("hx"), lax.axis_size("core")
    parts = chips * cores
    me = hx * cores + core
    other = 1 - core
    tokens = out_x.shape[0]
    columns = x.shape[1]
    heads = columns // HD
    qw = grad_q.shape[1]
    begin = ctx * tokens * parts + hx * BLOCK
    group = core * chips + j
    starts = starts_of(lengths)

    def cols(n, width):
        return pl.ds(pl.multiple_of(n * width, 128), width)

    def remote(src, dst, ssem, rsem, device):
        return pltpu.make_async_remote_copy(
            src_ref=src, dst_ref=dst, send_sem=ssem, recv_sem=rsem, device_id=device, device_id_type=MESH
        )

    def q_moves():
        moves = []
        for d in range(1, parts):
            p = lax.rem(me + d, parts)
            device = {"hx": p // cores, "core": lax.rem(p, cores)}
            moves.append(remote(grad_q.at[cols(p, tokens), :], out_q.at[:, cols(me, qw)], q_send.at[d], q_recv.at[d], device))
        own = pltpu.make_async_copy(grad_q.at[cols(me, tokens), :], out_q.at[:, cols(me, qw)], own_sem.at[chips, 0])
        return moves, own

    def pair_moves(n):
        moves, owns = [], []
        for k, (res, out, width) in enumerate(((res_x, out_x, columns), (res_w, out_w, NS), (res_r, out_r, NS))):
            place = out.at[:, cols(core * chips + n, width)]
            moves.append(
                remote(res.at[n, cols(other, tokens), :], place, pair_send.at[n, k], pair_recv.at[n, k], {"core": other})
            )
            owns.append(pltpu.make_async_copy(res.at[n, cols(core, tokens), :], place, own_sem.at[n, k]))
        return moves, owns

    @pl.when(j == 0)
    def _():
        barrier = pltpu.get_barrier_semaphore()
        for d in range(1, parts):
            p = lax.rem(me + d, parts)
            pl.semaphore_signal(
                barrier, inc=1, device_id={"hx": p // cores, "core": lax.rem(p, cores)}, device_id_type=MESH
            )
        pl.semaphore_wait(barrier, parts - 1)
        moves, own = q_moves()
        for c in moves + [own]:
            c.start()
        _, b, c, _ = edges(starts, begin, 0, st[...], rates_of(slow, fast, tokens * parts * lax.axis_size("ctx")))
        entering[...] = b
        to_end[...] = c

    spread = spread_matrix(columns, group)
    end_wide = widen(to_end[...], spread)
    iw = (x[...].astype(F32) * end_wide).astype(BF16)
    gw = (g[...].astype(F32) * widen(entering[...], spread)).astype(BF16)
    state = both[0, 0:columns, :]
    back = both[0, columns : 2 * columns, :]
    res_x[j] = (inner_x[...] + end_wide * dot_nt(w[...], back)).astype(BF16)
    res_w[j] = (inner_w[...] + dot_nn(iw, back)).astype(BF16)
    res_r[j] = (inner_r[...] + dot_nn(gw, state)).astype(BF16)

    for n in range(chips):

        @pl.when(j == n)
        def _():
            moves, owns = pair_moves(n)
            for c in moves + owns:
                c.start()

    @pl.when(j == chips - 1)
    def _():
        moves, own = q_moves()
        own.wait()
        for c in moves:
            c.wait_recv()
        for c in moves:
            c.wait_send()
        for n in range(chips):
            moves, owns = pair_moves(n)
            for c in owns:
                c.wait()
            for c in moves:
                c.wait_recv()
            for c in moves:
                c.wait_send()


def last_stage(lengths, slow, mix, fast, inner, both, grad_q, parts, cores):
    chips = both.shape[0]
    columns = both.shape[1] // 2
    tokens = BLOCK // cores
    groups = chips * cores
    hbm = pl.BlockSpec(memory_space=pltpu.HBM)
    dma = pltpu.SemaphoreType.DMA
    return pl.pallas_call(
        last_kernel,
        grid_spec=pltpu.PrefetchScalarGridSpec(
            num_scalar_prefetch=2,
            grid=(chips,),
            in_specs=[
                pl.BlockSpec((BLOCK, columns), lambda j, *_: (0, j)),
                pl.BlockSpec((BLOCK, columns), lambda j, *_: (0, j)),
                pl.BlockSpec((BLOCK, NS), lambda j, *_: (0, j)),
                pl.BlockSpec((BLOCK, 128), lambda j, *_: (0, 0)),
                pl.BlockSpec((1, 128), lambda j, *_: (0, 0)),
                pl.BlockSpec((BLOCK, columns), lambda j, *_: (0, j)),
                pl.BlockSpec((BLOCK, NS), lambda j, *_: (0, j)),
                pl.BlockSpec((BLOCK, NS), lambda j, *_: (0, j)),
                pl.BlockSpec((1, 2 * columns, NS), lambda j, *_: (j, 0, 0)),
                pl.BlockSpec(grad_q.shape, lambda j, *_: (0, 0)),
            ],
            out_specs=[hbm] * 4,
            scratch_shapes=[
                pltpu.VMEM((BLOCK, 128), F32),
                pltpu.VMEM((BLOCK, 128), F32),
                pltpu.VMEM((chips, BLOCK, columns), BF16),
                pltpu.VMEM((chips, BLOCK, NS), BF16),
                pltpu.VMEM((chips, BLOCK, NS), BF16),
                dma((chips + 1, 3)),
                dma((chips, 3)),
                dma((chips, 3)),
                dma((parts,)),
                dma((parts,)),
            ],
        ),
        out_shape=[
            jax.ShapeDtypeStruct((tokens, groups * columns), BF16),
            jax.ShapeDtypeStruct((tokens, groups * NS), BF16),
            jax.ShapeDtypeStruct((tokens, groups * NS), BF16),
            jax.ShapeDtypeStruct((tokens, parts * grad_q.shape[1]), BF16),
        ],
        compiler_params=pltpu.CompilerParams(vmem_limit_bytes=56 << 20, collective_id=1, has_side_effects=True),
        cost_estimate=pl.CostEstimate(flops=8 * 10**9, bytes_accessed=14 << 20, transcendentals=5 * 10**6),
        name="last_stage",
    )(lengths, slow, *mix, fast, *inner, both, grad_q)


HEAD = ("hx", "core")


def shards(x, w, r, steps, fast_rates, slow_heads, skip_gains, grad, q, k, v, ag, doc_lengths):
    parts = lax.axis_size(HEAD)
    cores = lax.axis_size("core")
    slab_first = (lax.axis_index("ctx") * x.shape[0] * parts).astype(jnp.int32).reshape(1)
    fast = fast_rates.reshape(1, MH)
    gains = skip_gains.reshape(1, MH)
    *mix, kv, qg, both = first_stage(
        doc_lengths, slow_heads, x, grad, w, r, steps, q, k, v, ag, fast, gains, parts, cores
    )
    mix, inner = mix[:4], mix[4:]
    both = lax.all_to_all(both, "hx", split_axis=0, concat_axis=0, tiled=True)
    grad_q = attention(qg, kv, doc_lengths, slab_first)
    return tuple(last_stage(doc_lengths, slow_heads, mix, fast, inner, both, grad_q, parts, cores))


def solution(mesh):
    split = Mesh(mesh.devices.reshape(mesh.shape["ctx"], -1, 2), ("ctx", "hx", "core"))
    tokens = P(("ctx", "hx", "core"), None)
    return jax.shard_map(
        shards,
        mesh=split,
        in_specs=(tokens, tokens, tokens, tokens, P(), P(), P(), tokens, tokens, tokens, tokens, tokens, P()),
        out_specs=(tokens, tokens, tokens, tokens),
        check_vma=False,
    )
```
